256 devices in a mesh: lon: 16 (over z, x_lo), lat: 16 (over x_hi, y, core).
Axes of the slice: x: 4 (x_hi: 2, x_lo: 2; x = x_hi * 2 + x_lo), y: 4, z: 8, core: 2. Of those that a mesh axis runs over, the one named last changes fastest.
Arguments:
- tracer: float32 [4, 12, 1024, 4096], P(None, None, 'lat', 'lon'), may hold values from -6 to 6
- east_velocity: float32 [12, 1024, 4096], P(None, 'lat', 'lon'), may hold values from -0.25 to 0.25
- north_velocity: float32 [12, 1024, 4096], P(None, 'lat', 'lon'), may hold values from -0.25 to 0.25
- diffusivity: float32 [12, 1024, 4096], P(None, 'lat', 'lon'), may hold values from 0.01 to 0.12
- east_slope: float32 [12, 1024, 4096], P(None, 'lat', 'lon'), may hold values from -0.5 to 0.5
- north_slope: float32 [12, 1024, 4096], P(None, 'lat', 'lon'), may hold values from -0.5 to 0.5
- vertical_diffusivity: float32 [11, 1024, 4096], P(None, 'lat', 'lon'), may hold values from 0.1 to 10
- sea_mask: int32 [12, 1024, 4096], P(None, 'lat', 'lon'), may hold values from 0 to 1, as said below
- bottom: int32 [1024, 4096], P('lat', 'lon'), may hold values from 0 to 12, as said below
Outputs:
- updated: float32 [4, 12, 1024, 4096], P(None, None, 'lat', 'lon')
The draws below stay inside these ranges and needn't reach their ends.
Inputs may be any that keep to these rules, and one draw needn't show every extreme that they name: sea_mask is 1 exactly at the levels k < bottom of its column. `bottom`: 0 marks a land column.
All inputs are finite; a program needn't handle non-finite values.
Results may differ from the reference program's by a relative error of at most 0.0003.
Values sent between devices are 32-bit elements; how exact they have to be, the bound alone decides.
No kernel may reach another device: no remote copies, remote signals or barrier semaphores. Data moves between devices by JAX's collectives and lax.ppermute only.
A program may use at most 128 MiB of HBM per device.

```python
import math
import jax
import jax.numpy as jnp
from jax import lax

NTR = 4
LEVELS = 12
NX = 4096
NY = 1024


def column_depths(key):
    return jax.random.randint(jax.random.fold_in(key, 11), (NY, NX), 0, LEVELS + 1).astype(jnp.int32)


def draw_bottom(key, part):
    return column_depths(key)


def draw_sea_mask(key, part):
    depths = column_depths(key)
    levels = jnp.arange(LEVELS).astype(jnp.int32)[:, None, None]
    return (levels < depths[None]).astype(jnp.int32)


def block_levels(key, dims, cuts, low, largest):
    level, own = 1.0, jax.random.fold_in(key, 6)
    for axis_at, shards_of in cuts:
        steps = jnp.exp(jax.random.uniform(jax.random.fold_in(own, axis_at), (shards_of,), jnp.float32, low / len(cuts), largest / len(cuts)))
        level = level * jnp.repeat(steps, dims[axis_at] // shards_of).reshape([-1 if axis == axis_at else 1 for axis in range(len(dims))])
    return level


def scatter_about(own_key, extent, deviation, bound, pieces=(), held_as=jnp.bfloat16):
    values = jax.random.normal(own_key, extent, jnp.float32) * deviation
    if len(pieces) > 0:
        values = block_levels(own_key, extent, pieces, -0.22, 0.18) * values
    return jnp.clip(values, min=-bound, max=bound).astype(held_as)


def setup_inputs(seed: int = 0) -> dict:
    key_list = jax.random.split(jax.random.key(seed), 10)
    tracer = scatter_about(key_list[0], (NTR, LEVELS, NY, NX), 1.0, 6.0, ((2, 16), (3, 16)), jnp.float32)
    east_velocity = jnp.clip(jax.random.uniform(key_list[1], (LEVELS, NY, NX), jnp.float32, -0.25, 0.25) * block_levels(key_list[1], (LEVELS, NY, NX), ((1, 16), (2, 16)), -0.4, 0.0), -0.25, 0.25)
    north_velocity = jnp.clip(jax.random.uniform(key_list[2], (LEVELS, NY, NX), jnp.float32, -0.25, 0.25) * block_levels(key_list[2], (LEVELS, NY, NX), ((1, 16), (2, 16)), -0.4, 0.0), -0.25, 0.25)
    diffusivity = jnp.clip(jnp.exp(math.log(0.12) - 2.4849066 * jax.random.uniform(key_list[3], (LEVELS, NY, NX), jnp.float32) ** block_levels(key_list[3], (LEVELS, NY, NX), ((1, 16), (2, 16)), -0.2, 0.2)), 0.01, 0.12)
    east_slope = jnp.clip(jax.random.uniform(key_list[4], (LEVELS, NY, NX), jnp.float32, -0.5, 0.5) * block_levels(key_list[4], (LEVELS, NY, NX), ((1, 16), (2, 16)), -0.4, 0.0), -0.5, 0.5)
    north_slope = jnp.clip(jax.random.uniform(key_list[5], (LEVELS, NY, NX), jnp.float32, -0.5, 0.5) * block_levels(key_list[5], (LEVELS, NY, NX), ((1, 16), (2, 16)), -0.4, 0.0), -0.5, 0.5)
    vertical_diffusivity = jnp.clip(jnp.exp(math.log(10.0) - 4.6051702 * jax.random.uniform(key_list[6], (LEVELS - 1, NY, NX), jnp.float32) ** block_levels(key_list[6], (LEVELS - 1, NY, NX), ((1, 16), (2, 16)), -0.2, 0.2)), 0.1, 10.0)
    sea_mask = draw_sea_mask(jax.random.fold_in(key_list[9], 71), 0)
    bottom = draw_bottom(jax.random.fold_in(key_list[9], 71), 0)
    return {"tracer": tracer, "east_velocity": east_velocity, "north_velocity": north_velocity, "diffusivity": diffusivity, "east_slope": east_slope, "north_slope": north_slope, "vertical_diffusivity": vertical_diffusivity, "sea_mask": sea_mask, "bottom": bottom}


def minmod(first, second):
    return 0.5 * (jnp.sign(first) + jnp.sign(second)) * jnp.minimum(jnp.abs(first), jnp.abs(second))


def vertical_slope(field):
    zeros = jnp.zeros_like(field[..., :1, :, :])
    padded = jnp.concatenate([zeros, field, zeros], axis=-3)
    return 0.5 * (padded[..., 2:, :, :] - padded[..., :-2, :, :])


def transport(concentration, mask, east_velocity, north_velocity, diffusivity, east_slope, north_slope):
    masked = concentration * mask
    slope_z = vertical_slope(masked)
    row_pad = masked[..., 2:-2, :]
    mask_rows = mask[..., 2:-2, :]
    east_open = mask_rows[..., :-1] * mask_rows[..., 1:]
    east_jump = (row_pad[..., 1:] - row_pad[..., :-1]) * east_open
    face_open = east_open[..., 1:-1]
    jump_here = east_jump[..., 1:-1]
    speed = east_velocity[..., 2:-2, 1:-2] * face_open
    upstream = jnp.where(speed >= 0, row_pad[..., 1:-2], row_pad[..., 2:-1])
    back = jnp.where(speed >= 0, east_jump[..., :-2], east_jump[..., 2:])
    flux = speed * upstream + 0.5 * jnp.abs(speed) * (1.0 - jnp.abs(speed)) * minmod(jump_here, back)
    slope_rows = slope_z[..., 2:-2, :]
    spread = 0.5 * (diffusivity[..., 2:-2, 1:-2] + diffusivity[..., 2:-2, 2:-1]) * (
        jump_here - 0.25 * east_slope[..., 2:-2, 1:-2] * face_open * (slope_rows[..., 1:-2] + slope_rows[..., 2:-1]))
    east_net = spread - flux
    col_pad = masked[..., :, 2:-2]
    mask_cols = mask[..., :, 2:-2]
    north_open = mask_cols[..., :-1, :] * mask_cols[..., 1:, :]
    north_jump = (col_pad[..., 1:, :] - col_pad[..., :-1, :]) * north_open
    face_north = north_open[..., 1:-1, :]
    jump_north = north_jump[..., 1:-1, :]
    speed_north = north_velocity[..., 1:-2, 2:-2] * face_north
    upstream_north = jnp.where(speed_north >= 0, col_pad[..., 1:-2, :], col_pad[..., 2:-1, :])
    back_north = jnp.where(speed_north >= 0, north_jump[..., :-2, :], north_jump[..., 2:, :])
    flux_north = speed_north * upstream_north + 0.5 * jnp.abs(speed_north) * (1.0 - jnp.abs(speed_north)) * minmod(jump_north, back_north)
    slope_cols = slope_z[..., :, 2:-2]
    spread_north = 0.5 * (diffusivity[..., 1:-2, 2:-2] + diffusivity[..., 2:-1, 2:-2]) * (
        jump_north - 0.25 * north_slope[..., 1:-2, 2:-2] * face_north * (slope_cols[..., 1:-2, :] + slope_cols[..., 2:-1, :]))
    north_net = spread_north - flux_north
    change = (east_net[..., 1:] - east_net[..., :-1]) + (north_net[..., 1:, :] - north_net[..., :-1, :])
    return (masked[..., 2:-2, 2:-2] + change) * mask[..., 2:-2, 2:-2]


def vertical_mix(explicit, vertical_diffusivity, bottom):
    levels = explicit.shape[-3]
    interface = jnp.arange(1, levels).astype(jnp.int32)[:, None, None]
    weights = jnp.where(interface < bottom[None], vertical_diffusivity, jnp.zeros_like(vertical_diffusivity))
    zero_level = jnp.zeros_like(weights[:1])
    above = jnp.concatenate([zero_level, weights], axis=0)
    below = jnp.concatenate([weights, zero_level], axis=0)
    diagonal = 1.0 + above + below
    right_side = jnp.moveaxis(explicit, -3, 0)

    def forward(carry, items):
        ratio_prev, value_prev = carry
        above_k, diagonal_k, below_k, right_k = items
        pivot = diagonal_k - above_k * ratio_prev
        ratio_now = -below_k / pivot
        value_now = (right_k + above_k * value_prev) / pivot
        return (ratio_now, value_now), (ratio_now, value_now)

    start = (jnp.zeros_like(diagonal[0]), jnp.zeros_like(right_side[0]))
    _, (ratios, values) = lax.scan(forward, start, (above, diagonal, below, right_side))

    def backward(next_value, items):
        ratio_k, value_k = items
        result = value_k - ratio_k * next_value
        return result, result

    _, solved = lax.scan(backward, jnp.zeros_like(right_side[0]), (ratios, values), reverse=True)
    return jnp.moveaxis(solved, 0, -3)


def pad_field(field):
    ghost = field[..., -2:, :][..., ::-1, ::-1]
    south = jnp.zeros_like(field[..., :2, :])
    stacked_rows = jnp.concatenate([south, field, ghost], axis=-2)
    return jnp.concatenate([stacked_rows[..., -2:], stacked_rows, stacked_rows[..., :2]], axis=-1)


def reference(tracer, east_velocity, north_velocity, diffusivity, east_slope, north_slope, vertical_diffusivity, sea_mask, bottom):
    mask_float = sea_mask.astype(jnp.float32)
    top_row = north_velocity[:, -1, :]
    folded = north_velocity.at[:, -1, :].set(0.5 * (top_row - top_row[:, ::-1]))
    padded = [pad_field(field) for field in (mask_float, east_velocity, folded, diffusivity, east_slope, north_slope)]

    def single(concentration):
        explicit = transport(pad_field(concentration), *padded)
        return vertical_mix(explicit, vertical_diffusivity, bottom)

    return lax.map(single, tracer)
```

```python
import jax
import jax.numpy as jnp
from jax import lax
from jax.experimental import pallas as pl
from jax.experimental.pallas import tpu as pltpu
from jax.sharding import PartitionSpec as P

F32 = jnp.float32
LANES = 128
ROWS = 8


def iota(shape, dim):
    return lax.broadcasted_iota(jnp.int32, shape, dim)


def minmod(first, second):
    return jnp.minimum(
        jnp.maximum(second, jnp.minimum(first, 0.0)), jnp.maximum(first, 0.0)
    )


def limiter_weight(speed):
    size = jnp.abs(speed)
    return 0.5 * size * (1.0 - size)


def pack_kernel(levels, tracers, rows, cols, lon_name, lat_name, *refs):
    (
        tracer_hbm,
        east_vel_hbm,
        north_vel_hbm,
        diff_hbm,
        east_slope_hbm,
        north_slope_hbm,
        bottom_hbm,
        pay_a,
        pay_b,
        pay_c,
        pay_d,
        own_lon,
        own_lat,
        own_lat_coef,
        tracer_v,
        east_vel_v,
        diff_v,
        east_slope_v,
        north_v,
        bottom_v,
        sems,
        row_sems,
    ) = refs
    items = levels * tracers
    group = 3
    groups = levels // group
    last = rows - ROWS
    copies = []
    row_copies = [pltpu.make_async_copy(bottom_hbm, bottom_v, row_sems.at[0])]
    for n, (src, start) in enumerate(
        ((north_vel_hbm, 0), (north_vel_hbm, last), (north_slope_hbm, 0), (north_slope_hbm, last))
    ):
        row_copies.append(
            pltpu.make_async_copy(
                src.at[:, pl.ds(start, ROWS), :], north_v.at[n], row_sems.at[n + 1]
            )
        )
    for g in range(groups):
        span = pl.ds(g * group, group)
        fetch = [
            pltpu.make_async_copy(
                tracer_hbm.at[:, span], tracer_v.at[:, span], sems.at[g, 0]
            )
        ]
        for n, (src, dst) in enumerate(
            ((diff_hbm, diff_v), (east_vel_hbm, east_vel_v), (east_slope_hbm, east_slope_v))
        ):
            fetch.append(pltpu.make_async_copy(src.at[span], dst.at[span], sems.at[g, n + 1]))
        copies.append(fetch)
    for copy in copies[0]:
        copy.start()
    for copy in row_copies:
        copy.start()
    for fetch in copies[1:]:
        for copy in fetch:
            copy.start()

    lane = iota((rows, LANES), 1)
    sub = iota((ROWS, cols), 0)
    right = cols - LANES
    zero = jnp.zeros((rows, LANES), F32)
    cells = [zero] * 6
    d_cols, v_cols, s_cols = [zero] * 4, [zero] * 3, [zero] * 3
    row_at = (0, 1, 2, rows - 3, rows - 2, rows - 1)
    for copy in row_copies:
        copy.wait()
    row_bottoms = [bottom_v[r : r + 1, :] for r in row_at]
    block = [[jnp.zeros((ROWS, cols), F32)] * 6 for _ in range(items // ROWS)]
    edge_bottom = jnp.where(lane < 64, bottom_v[:, :LANES], bottom_v[:, right:])

    def ends(ref, index):
        return jnp.where(lane < 64, ref[index][:, :LANES], ref[index][:, right:])

    for g in range(groups):
        for copy in copies[g]:
            copy.wait()
        for k in range(g * group, (g + 1) * group):
            sea = edge_bottom > k
            for t in range(tracers):
                n = k * tracers + t
                both = jnp.where(sea, jnp.where(
                    lane < 64, tracer_v[t, k, :, :LANES], tracer_v[t, k, :, right:]), 0.0)
                turned = pltpu.roll(both, n, axis=1) if n else both
                for c in range(6):
                    place = (n + (c if c < 3 else c - 6)) % LANES
                    cells[c] = jnp.where(lane == place, turned, cells[c])
                for c, r in enumerate(row_at):
                    row = jnp.where(row_bottoms[c] > k, tracer_v[t, k, r : r + 1, :], 0.0)
                    block[n // ROWS][c] = jnp.where(
                        sub == n % ROWS, jnp.broadcast_to(row, (ROWS, cols)), block[n // ROWS][c]
                    )
            n = k * tracers
            for ref, outs, places in (
                (diff_v, d_cols, (0, 1, -2, -1)),
                (east_vel_v, v_cols, (0, -2, -1)),
                (east_slope_v, s_cols, (0, -2, -1)),
            ):
                both = jnp.where(lane < 64, ref[k, :, :LANES], ref[k, :, right:])
                turned = pltpu.roll(both, n, axis=1) if n else both
                for c, off in enumerate(places):
                    outs[c] = jnp.where(lane == (n + off) % LANES, turned, outs[c])
    cells = [
        x if c == 0 else pltpu.roll(x, (-(c if c < 3 else c - 6)) % LANES, axis=1)
        for c, x in enumerate(cells)
    ]

    def spread(x, off):
        x = pltpu.roll(x, (-off) % LANES, axis=1) if off else x
        x = x + pltpu.roll(x, 1, axis=1)
        return x + pltpu.roll(x, 2, axis=1)

    d_cols = [spread(x, off) for x, off in zip(d_cols, (0, 1, -2, -1))]
    v_cols = [spread(x, off) for x, off in zip(v_cols, (0, -2, -1))]
    s_cols = [spread(x, off) for x, off in zip(s_cols, (0, -2, -1))]
    level_of = lane // tracers

    def column_mask(c):
        col = bottom_v[:, c : c + 1] if c >= 0 else bottom_v[:, cols + c : cols + c + 1]
        ok = (level_of < jnp.broadcast_to(col, (rows, LANES))) & (lane < items)
        return jnp.where(ok, 1.0, 0.0)

    m = [column_mask(c) for c in (0, 1, 2, -3, -2, -1)]
    jump_01 = (cells[1] - cells[0]) * (m[0] * m[1])
    jump_12 = (cells[2] - cells[1]) * (m[1] * m[2])
    jump_e0 = (cells[4] - cells[3]) * (m[3] * m[4])
    jump_e1 = (cells[5] - cells[4]) * (m[4] * m[5])

    def pair(low, high):
        return low + pltpu.roll(high, 64, axis=1)

    odd_lon = lax.rem(lax.axis_index(lon_name), 2) == 1
    odd_lat = lax.rem(lax.axis_index(lat_name), 2) == 1
    east = (pair(cells[5], jump_e1), pair(d_cols[3], v_cols[2]), pair(s_cols[2], m[5]))
    west = (pair(cells[0], jump_01), pair(d_cols[0], zero), pair(zero, m[0]))
    for n in range(3):
        pay_c[n] = jnp.where(odd_lon, west[n], east[n])
        pay_d[n] = jnp.where(odd_lon, east[n], west[n])
    for n, x in enumerate(
        [cells[0], cells[1], jump_12, cells[4], cells[5], jump_e0] + d_cols + v_cols + s_cols
    ):
        own_lon[n] = x

    for b in range(items // ROWS):
        at = pl.ds(b * ROWS, ROWS)
        level = (sub + b * ROWS) // tracers
        m = [
            jnp.where(level < jnp.broadcast_to(x, (ROWS, cols)), 1.0, 0.0) for x in row_bottoms
        ]
        x = block[b]
        j01 = (x[1] - x[0]) * (m[0] * m[1])
        j12 = (x[2] - x[1]) * (m[1] * m[2])
        k0 = (x[4] - x[3]) * (m[3] * m[4])
        k1 = (x[5] - x[4]) * (m[4] * m[5])
        for n, y in enumerate((x[0], x[1], j12, x[4], x[5], k0)):
            own_lat[n, at, :] = y
        pay_a[at, :] = jnp.where(odd_lat, x[0], x[5])
        pay_b[at, :] = jnp.where(odd_lat, x[5], x[0])
        at = pl.ds(items + b * ROWS, ROWS)
        pay_a[at, :] = jnp.where(odd_lat, j01, k1)
        pay_b[at, :] = jnp.where(odd_lat, k1, j01)
    base = 2 * items
    for k in range(levels):
        values = (
            diff_v[k, 0:1, :],
            diff_v[k, 1:2, :],
            diff_v[k, rows - 2 : rows - 1, :],
            diff_v[k, rows - 1 : rows, :],
            north_v[0, k, 0:1, :],
            north_v[1, k, 6:7, :],
            north_v[1, k, 7:8, :],
            north_v[2, k, 0:1, :],
            north_v[3, k, 6:7, :],
            north_v[3, k, 7:8, :],
        )
        for n, y in enumerate(values):
            own_lat_coef[n, k : k + 1, :] = y
        for n, top in enumerate((values[3], values[6], values[9])):
            low = values[0] if n == 0 else jnp.zeros_like(top)
            r = base + n * levels + k
            pay_a[r : r + 1, :] = jnp.where(odd_lat, low, top)
            pay_b[r : r + 1, :] = jnp.where(odd_lat, top, low)
    r = base + 3 * levels
    low, top = row_bottoms[0].astype(F32), row_bottoms[5].astype(F32)
    pay_a[r : r + 1, :] = jnp.where(odd_lat, low, top)
    pay_b[r : r + 1, :] = jnp.where(odd_lat, top, low)
    for q in range(r + 1, pay_a.shape[0]):
        pay_a[q : q + 1, :] = jnp.zeros_like(low)
        pay_b[q : q + 1, :] = jnp.zeros_like(low)


def pack(tracer, east_vel, north_vel, diff, east_slope, north_slope, bottom):
    tracers, levels, rows, cols = tracer.shape
    items = tracers * levels
    lat_rows = -(-(2 * items + 3 * levels + 1) // ROWS) * ROWS
    shape = jax.ShapeDtypeStruct
    vmem = pl.BlockSpec(memory_space=pltpu.VMEM)

    def body(*refs):
        pack_kernel(levels, tracers, rows, cols, "lon", "lat", *refs)

    return pl.pallas_call(
        body,
        name="pack_edges",
        in_specs=[pl.BlockSpec(memory_space=pltpu.HBM)] * 7,
        out_specs=[vmem] * 7,
        out_shape=[
            shape((lat_rows, cols), F32),
            shape((lat_rows, cols), F32),
            shape((3, rows, LANES), F32),
            shape((3, rows, LANES), F32),
            shape((16, rows, LANES), F32),
            shape((6, items, cols), F32),
            shape((10, levels, cols), F32),
        ],
        scratch_shapes=[
            pltpu.VMEM((tracers, levels, rows, cols), F32),
            pltpu.VMEM((levels, rows, cols), F32),
            pltpu.VMEM((levels, rows, cols), F32),
            pltpu.VMEM((levels, rows, cols), F32),
            pltpu.VMEM((4, levels, ROWS, cols), F32),
            pltpu.VMEM((rows, cols), jnp.int32),
            pltpu.SemaphoreType.DMA((levels // 3, 4)),
            pltpu.SemaphoreType.DMA((5,)),
        ],
        compiler_params=pltpu.CompilerParams(vmem_limit_bytes=24 << 20),
        cost_estimate=pl.CostEstimate(flops=10**6, bytes_accessed=7 * 10**6, transcendentals=0),
    )(tracer, east_vel, north_vel, diff, east_slope, north_slope, bottom)


def interior_kernel(levels, tracers, rows, cols, *refs):
    (
        tracer,
        east_vel,
        north_vel,
        diff,
        east_slope,
        north_slope,
        bottom,
        explicit,
        ring,
        open_at,
        coef,
    ) = refs
    step = pl.program_id(0)
    blocks = rows // ROWS
    halves = (slice(0, LANES), slice(LANES, 2 * LANES))
    lane = iota((ROWS, LANES), 1)
    sub = iota((ROWS, LANES), 0)

    def chunk(b):
        return slice(b * ROWS, (b + 1) * ROWS)

    def east_of(x):
        left, right = x
        turned = pltpu.roll(right, LANES - 1, axis=1)
        return (
            jnp.where(lane == LANES - 1, turned, pltpu.roll(left, LANES - 1, axis=1)),
            turned,
        )

    def west_of(x):
        left, right = x
        turned = pltpu.roll(left, 1, axis=1)
        return turned, jnp.where(lane == 0, turned, pltpu.roll(right, 1, axis=1))

    def up(x):
        return tuple(pltpu.roll(y, ROWS - 1, axis=0) for y in x)

    def down(x):
        return tuple(pltpu.roll(y, 1, axis=0) for y in x)

    def north_of(turned, turned_next):
        if turned_next is None:
            return turned
        return tuple(jnp.where(sub == ROWS - 1, n, y) for y, n in zip(turned, turned_next))

    def south_of(turned, turned_before):
        if turned_before is None:
            return turned
        return tuple(jnp.where(sub == 0, n, y) for y, n in zip(turned, turned_before))

    def load(ref, *index):
        *lead, b = index
        return tuple(ref[(*lead, chunk(b), h)] for h in halves)

    @pl.when(step == 0)
    def _():
        ring[2] = jnp.zeros(ring.shape[1:], F32)
        for b in range(blocks):
            here = load(bottom, b)
            nxt = load(bottom, min(b + 1, blocks - 1))
            east = tuple(jnp.minimum(x, y) for x, y in zip(here, east_of(here)))
            north = tuple(
                jnp.minimum(x, y) for x, y in zip(here, north_of(up(here), up(nxt)))
            )
            row = sub + b * ROWS
            for i, h in enumerate(halves):
                col = lane + i * LANES
                open_at[0, chunk(b), h] = east[i]
                open_at[1, chunk(b), h] = jnp.where(
                    (col == 0) | (col >= cols - 2), 0, east[i]
                )
                open_at[2, chunk(b), h] = north[i]
                open_at[3, chunk(b), h] = jnp.where(
                    (row == 0) | (row >= rows - 2), 0, north[i]
                )

    @pl.when(step < levels)
    def _():
        slot = lax.rem(step, 3)
        for b in range(blocks):
            sea = tuple(x > step for x in load(bottom, b))
            for t in range(tracers):
                for i, h in enumerate(halves):
                    ring[slot, t, chunk(b), h] = jnp.where(sea[i], tracer[t, 0, chunk(b), h], 0.0)

    @pl.when(step == levels)
    def _():
        ring[levels % 3] = jnp.zeros(ring.shape[1:], F32)

    @pl.when(step > 0)
    def _():
        level = step - 1
        slot, above, below = lax.rem(step + 2, 3), lax.rem(step + 1, 3), lax.rem(step, 3)
        for b in range(blocks):
            here = load(diff, 0, b)
            north = north_of(up(here), up(load(diff, 0, min(b + 1, blocks - 1))))
            for way, other, vel, slope in (
                (0, east_of(here), east_vel, east_slope),
                (1, north, north_vel, north_slope),
            ):
                for i, h in enumerate(halves):
                    at = (chunk(b), h)
                    free = open_at[(2 * way, *at)] > level
                    face = open_at[(2 * way + 1, *at)] > level
                    speed = jnp.where(face, vel[(0, *at)], 0.0)
                    mean = jnp.where(face, 0.5 * (here[i] + other[i]), 0.0)
                    coef[(5 * way, *at)] = jnp.where(free, 1.0, 0.0)
                    coef[(5 * way + 1, *at)] = speed
                    coef[(5 * way + 2, *at)] = limiter_weight(speed)
                    coef[(5 * way + 3, *at)] = mean
                    coef[(5 * way + 4, *at)] = 0.125 * slope[(0, *at)] * mean

        def face(way, b, here, other, jump, bend, bend_other, tilt):
            out = []
            for i, h in enumerate(halves):
                at = (chunk(b), h)
                speed = coef[(5 * way + 1, *at)]
                ahead = speed >= 0
                upstream = jnp.where(ahead, here[i], other[i])
                limited = jnp.where(ahead, bend[i], bend_other[i])
                out.append(
                    (coef[(5 * way + 3, *at)] * jump[i] - coef[(5 * way + 4, *at)] * tilt[i])
                    - (speed * upstream + coef[(5 * way + 2, *at)] * limited)
                )
            return tuple(out)

        def sub2(x, y):
            return tuple(p - q for p, q in zip(x, y))

        def add2(x, y):
            return tuple(p + q for p, q in zip(x, y))

        def mul2(x, y):
            return tuple(p * q for p, q in zip(x, y))

        def one(t, carry):
            def stage(b):
                here = load(ring, slot, t, b)
                tilt = sub2(load(ring, below, t, b), load(ring, above, t, b))
                return here, up(here), tilt, up(tilt)

            now = stage(0)
            jump_before = bend_turned = flux_before = None
            held = None
            for b in range(blocks + 1):
                if b < blocks:
                    nxt = stage(b + 1) if b + 1 < blocks else (None,) * 4
                    here, turned, tilt, tilt_turned = now
                    north = north_of(turned, nxt[1])
                    step_n = sub2(north, here)
                    jump = mul2(step_n, load(coef, 5, b))
                    jump_turned = down(jump)
                    bend = tuple(
                        minmod(x, y) for x, y in zip(jump, south_of(jump_turned, jump_before))
                    )
                    bend_turned = up(bend)
                    jump_before = jump_turned
                if held is not None:
                    pb, p_here, p_north, p_step, p_bend, p_bend_turned, p_tilt, p_tilt_n = held
                    bend_n = north_of(p_bend_turned, bend_turned if b < blocks else None)
                    flux = face(
                        1, pb, p_here, p_north, p_step, p_bend, bend_n, add2(p_tilt, p_tilt_n)
                    )
                    flux_turned = down(flux)
                    if flux_before is None:
                        flux_s = tuple(jnp.where(sub == 0, 0.0, y) for y in flux_turned)
                    else:
                        flux_s = south_of(flux_turned, flux_before)
                    flux_before = flux_turned
                    total = add2(p_here, sub2(flux, flux_s))
                    east = east_of(p_here)
                    step_e = sub2(east, p_here)
                    jump_e = mul2(step_e, load(coef, 0, pb))
                    bend_e = tuple(minmod(x, y) for x, y in zip(jump_e, west_of(jump_e)))
                    flux_e = face(
                        0,
                        pb,
                        p_here,
                        east,
                        step_e,
                        bend_e,
                        east_of(bend_e),
                        add2(p_tilt, east_of(p_tilt)),
                    )
                    left, right = west_of(flux_e)
                    flux_w = (jnp.where(lane == 0, 0.0, left), right)
                    total = add2(total, sub2(flux_e, flux_w))
                    for i, h in enumerate(halves):
                        explicit[t, 0, chunk(pb), h] = total[i]
                if b < blocks:
                    tilt_n = north_of(tilt_turned, nxt[3])
                    held = (b, here, north, step_n, bend, bend_turned, tilt, tilt_n)
                    now = nxt
            return carry

        lax.fori_loop(0, tracers, one, 0)


def interior(tracer, east_vel, north_vel, diff, east_slope, north_slope, bottom):
    tracers, levels, rows, cols = tracer.shape

    def body(*refs):
        interior_kernel(levels, tracers, rows, cols, *refs)

    flat = pl.BlockSpec((1, rows, cols), lambda s: (jnp.maximum(s - 1, 0), 0, 0))
    return pl.pallas_call(
        body,
        name="interior_faces",
        grid=(levels + 1,),
        in_specs=[
            pl.BlockSpec(
                (tracers, 1, rows, cols), lambda s: (0, jnp.minimum(s, levels - 1), 0, 0)
            ),
            flat,
            flat,
            flat,
            flat,
            flat,
            pl.BlockSpec((rows, cols), lambda s: (0, 0)),
        ],
        out_specs=pl.BlockSpec(
            (tracers, 1, rows, cols), lambda s: (0, jnp.maximum(s - 1, 0), 0, 0)
        ),
        out_shape=jax.ShapeDtypeStruct(tracer.shape, F32),
        scratch_shapes=[
            pltpu.VMEM((3, tracers, rows, cols), F32),
            pltpu.VMEM((4, rows, cols), jnp.int32),
            pltpu.VMEM((10, rows, cols), F32),
        ],
        compiler_params=pltpu.CompilerParams(
            dimension_semantics=("arbitrary",), vmem_limit_bytes=16 << 20
        ),
        cost_estimate=pl.CostEstimate(
            flops=60 * tracer.size, bytes_accessed=12 * 10**6, transcendentals=0
        ),
    )(tracer, east_vel, north_vel, diff, east_slope, north_slope, bottom)


def edge_faces(m1, m2, m3, j0, j3, open1, open2, d1, d2, d3, v0, v1, s0, s1, tilt):
    j1 = (m2 - m1) * open1
    j2 = (m3 - m2) * open2
    t1, t2, t3 = tilt(m1), tilt(m2), tilt(m3)

    def face(low, high, behind, jump, ahead, opened, d_sum, vel, slope, tilts):
        speed = vel * opened
        forward = speed >= 0
        flux = speed * jnp.where(forward, low, high) + limiter_weight(speed) * minmod(
            jump, jnp.where(forward, behind, ahead)
        )
        return 0.5 * d_sum * (jump - 0.125 * slope * opened * tilts) - flux

    return (
        face(m1, m2, j0, j1, j2, open1, d1 + d2, v0, s0, t1 + t2),
        face(m2, m3, j1, j2, j3, open2, d2 + d3, v1, s1, t2 + t3),
    )


def solve_kernel(levels, tracers, rows, cols, lon_name, lat_name, lat_count, *refs):
    (
        explicit,
        vertical,
        bottom,
        got_a,
        got_b,
        got_c,
        got_d,
        own_lon,
        own_lat,
        own_lat_coef,
        out,
        fix_lon,
        fix_lat,
        south,
        north,
        pivots,
        solved,
    ) = refs
    step = pl.program_id(0)
    blocks = rows // ROWS
    items = levels * tracers
    base = 2 * items
    halves = (slice(0, LANES), slice(LANES, 2 * LANES))
    lane = iota((ROWS, LANES), 1)
    sub = iota((ROWS, LANES), 0)

    @pl.when(step == 0)
    def _():
        odd_lon = lax.rem(lax.axis_index(lon_name), 2) == 1
        lat = lax.axis_index(lat_name)
        odd_lat = lax.rem(lat, 2) == 1
        top = lat == lat_count - 1
        item = iota((ROWS, LANES), 1)
        inside = item < items
        level = item // tracers

        def tilt_lanes(x):
            return pltpu.roll(x, LANES - tracers, axis=1) - pltpu.roll(x, tracers, axis=1)

        for b in range(blocks):
            at = slice(b * ROWS, (b + 1) * ROWS)

            def mask(c):
                col = jnp.broadcast_to(bottom[at, c : c + 1], (ROWS, LANES))
                return jnp.where((level < col) & inside, 1.0, 0.0)

            def halves_of(pays):
                low, high = [], []
                for x in pays:
                    low.append(jnp.where(inside, x, 0.0))
                    high.append(jnp.where(inside, pltpu.roll(x, 64, axis=1), 0.0))
                return low, high

            c_got = [got_c[n, at, :] for n in range(3)]
            d_got = [got_d[n, at, :] for n in range(3)]
            from_west = [jnp.where(odd_lon, c, d) for c, d in zip(c_got, d_got)]
            from_east = [jnp.where(odd_lon, d, c) for c, d in zip(c_got, d_got)]
            own = [own_lon[n, at, :] for n in range(16)]
            (wm, wd, ws), (wj, wv, wk) = halves_of(from_west)
            m0, m1 = mask(0), mask(1)
            f0, f1 = edge_faces(
                wm, own[0], own[1], wj, own[2], wk * m0, m0 * m1,
                wd, own[6], own[7], wv, own[10], ws, own[13], tilt_lanes,
            )
            fix_lon[0, at, :] = (f1 - f0) * m0
            fix_lon[1, at, :] = -f1 * m1
            (em, ed, _), (ej, _, ek) = halves_of(from_east)
            m0, m1 = mask(cols - 2), mask(cols - 1)
            f0, f1 = edge_faces(
                own[3], own[4], em, own[5], ej, m0 * m1, m1 * ek,
                own[8], own[9], ed, own[11], own[12], own[14], own[15], tilt_lanes,
            )
            fix_lon[2, at, :] = f0 * m0
            fix_lon[3, at, :] = (f1 - f0) * m1

        south[...] = jnp.where(odd_lat, got_a[...], got_b[...])

        @pl.when(jnp.logical_not(top))
        def _():
            north[...] = jnp.where(odd_lat, got_b[...], got_a[...])

        @pl.when(top)
        def _():
            for b in range(north.shape[0] // ROWS):
                at = slice(b * ROWS, (b + 1) * ROWS)
                for i in range(2):
                    x = got_b[at, halves[1 - i]]
                    for bit in range(7):
                        size = 1 << bit
                        x = jnp.where(
                            (lane & size) != 0,
                            pltpu.roll(x, size, axis=1),
                            pltpu.roll(x, LANES - size, axis=1),
                        )
                    north[at, halves[i]] = x

        wide = iota((ROWS, cols), 0)
        sign = jnp.where(top, -1.0, 1.0)

        def spread_rows(ref, first, b):
            k = b * ROWS // tracers
            low, high = ref[first + k : first + k + 1, :], ref[first + k + 1 : first + k + 2, :]
            return jnp.where(
                wide < tracers,
                jnp.broadcast_to(low, (ROWS, cols)),
                jnp.broadcast_to(high, (ROWS, cols)),
            )

        def tilt_rows_of(read):
            def tilt(b):
                here = read(b)
                zeros = jnp.zeros_like(here)
                turned = pltpu.roll(here, tracers, axis=0)
                after = pltpu.roll(read(b + 1), tracers, axis=0) if b + 1 < items // ROWS else zeros
                before = pltpu.roll(read(b - 1), tracers, axis=0) if b else zeros
                return jnp.where(wide < tracers, turned, after) - jnp.where(
                    wide < tracers, before, turned
                )

            return tilt

        def own_row(n):
            return lambda b: own_lat[n, b * ROWS : (b + 1) * ROWS, :]

        def ghost_row(ref):
            return lambda b: ref[b * ROWS : (b + 1) * ROWS, :]

        for b in range(items // ROWS):
            at = slice(b * ROWS, (b + 1) * ROWS)
            past = slice(items + b * ROWS, items + (b + 1) * ROWS)
            level = (wide + b * ROWS) // tracers

            def mask(row):
                return jnp.where(level < jnp.broadcast_to(row, (ROWS, cols)), 1.0, 0.0)

            def coef(n):
                return spread_rows(own_lat_coef.at[n], 0, b)

            def ghost_mask(ref):
                row = ref[base + 3 * levels : base + 3 * levels + 1, :]
                return jnp.where(level.astype(F32) < jnp.broadcast_to(row, (ROWS, cols)), 1.0, 0.0)

            def run(reads, j0, j3, open1, open2, d, v, s):
                tilts = [tilt_rows_of(r)(b) for r in reads]
                values = [r(b) for r in reads]
                lookup = dict(zip(map(id, values), tilts))
                return edge_faces(*values, j0, j3, open1, open2, *d, *v, *s,
                                  lambda x: lookup[id(x)])

            m0, m1 = mask(bottom[0:1, :]), mask(bottom[1:2, :])
            f0, f1 = run(
                (ghost_row(south), own_row(0), own_row(1)),
                south[past, :], own_lat[2, at, :], ghost_mask(south) * m0, m0 * m1,
                (spread_rows(south, base, b), coef(0), coef(1)),
                (spread_rows(south, base + levels, b), coef(4)),
                (spread_rows(south, base + 2 * levels, b), coef(7)),
            )
            fix_lat[0, at, :] = (f1 - f0) * m0
            fix_lat[1, at, :] = -f1 * m1
            m0 = mask(bottom[rows - 2 : rows - 1, :])
            m1 = mask(bottom[rows - 1 : rows, :])
            top_vel = coef(6)
            ghost_vel = spread_rows(north, base + levels, b)
            top_vel = jnp.where(top, 0.5 * (top_vel - ghost_vel), top_vel)
            f0, f1 = run(
                (own_row(3), own_row(4), ghost_row(north)),
                own_lat[5, at, :], sign * north[past, :], m0 * m1, m1 * ghost_mask(north),
                (coef(2), coef(3), spread_rows(north, base, b)),
                (coef(5), top_vel),
                (coef(8), coef(9)),
            )
            fix_lat[2, at, :] = f0 * m0
            fix_lat[3, at, :] = (f1 - f0) * m1

    depth = tuple(bottom[pl.ds(pl.multiple_of(step * ROWS, ROWS), ROWS), h] for h in halves)
    for i, h in enumerate(halves):
        ratio = above = None
        for k in range(levels):
            if k + 1 < levels:
                below = jnp.where(depth[i] > k + 1, vertical[k, :, h], 0.0)
            if k == 0:
                pivot = 1.0 + below
            elif k + 1 < levels:
                pivot = (1.0 + above + below) + above * ratio
            else:
                pivot = (1.0 + above) + above * ratio
            inverse = 1.0 / pivot
            pivots[0, k, :, h] = inverse
            if k:
                pivots[1, k, :, h] = above
            if k + 1 < levels:
                ratio = below * inverse
                pivots[2, k, :, h] = ratio
                above = below

    first_block = step == 0
    last_block = step == blocks - 1
    row0 = jnp.where(first_block, 0, ROWS - 2)
    pick = jnp.where(first_block, 0, 2)

    @pl.when(first_block | last_block)
    def _():
        for t in range(tracers):
            for k in range(levels):
                n = k * tracers + t
                for i, h in enumerate(halves):
                    low = fix_lat[pick, n : n + 1, h]
                    high = fix_lat[pick + 1, n : n + 1, h]
                    explicit_fix = jnp.where(
                        sub == row0,
                        jnp.broadcast_to(low, (ROWS, LANES)),
                        jnp.where(
                            sub == row0 + 1, jnp.broadcast_to(high, (ROWS, LANES)), 0.0
                        ),
                    )
                    solved[t, k, :, h] = explicit_fix

    @pl.when(jnp.logical_not(first_block | last_block))
    def _():
        solved[...] = jnp.zeros(solved.shape, F32)

    at = pl.ds(pl.multiple_of(step * ROWS, ROWS), ROWS)
    fixes = [fix_lon[n, at, :] for n in range(4)]
    for t in range(tracers):
        for i, h in enumerate(halves):
            a, b = fixes[2 * i], fixes[2 * i + 1]
            at_a, at_b = (0, 1) if i == 0 else (LANES - 2, LANES - 1)
            values = []
            value = None
            for k in range(levels):
                n = k * tracers + t
                patch = jnp.where(
                    lane == at_a,
                    pltpu.roll(a, (at_a - n) % LANES, axis=1),
                    jnp.where(lane == at_b, pltpu.roll(b, (at_b - n) % LANES, axis=1), 0.0),
                )
                right = (explicit[t, k, :, h] + solved[t, k, :, h]) + patch
                right = jnp.where(depth[i] > k, right, 0.0)
                if k:
                    right = right + pivots[1, k, :, h] * value
                value = right * pivots[0, k, :, h]
                values.append(value)
            nxt = values[-1]
            out[t, levels - 1, :, h] = nxt
            for k in range(levels - 2, -1, -1):
                nxt = values[k] + pivots[2, k, :, h] * nxt
                out[t, k, :, h] = nxt


def solve(explicit, vertical, bottom, got, own):
    tracers, levels, rows, cols = explicit.shape
    items = levels * tracers
    lat_rows = got[0].shape[0]
    lat_count = lax.axis_size("lat")

    def body(*refs):
        solve_kernel(levels, tracers, rows, cols, "lon", "lat", lat_count, *refs)

    whole = [
        pl.BlockSpec(x.shape, lambda s, n=x.ndim: (0,) * n, pipeline_mode=pl.Buffered(1))
        for x in (bottom, *got, *own)
    ]
    block = pl.BlockSpec((tracers, levels, ROWS, cols), lambda s: (0, 0, s, 0))
    return pl.pallas_call(
        body,
        name="edges_and_solve",
        grid=(rows // ROWS,),
        in_specs=[block, pl.BlockSpec((levels - 1, ROWS, cols), lambda s: (0, s, 0)), *whole],
        out_specs=block,
        out_shape=jax.ShapeDtypeStruct(explicit.shape, F32),
        scratch_shapes=[
            pltpu.VMEM((4, rows, LANES), F32),
            pltpu.VMEM((4, items, cols), F32),
            pltpu.VMEM((lat_rows, cols), F32),
            pltpu.VMEM((lat_rows, cols), F32),
            pltpu.VMEM((3, levels, ROWS, cols), F32),
            pltpu.VMEM((tracers, levels, ROWS, cols), F32),
        ],
        compiler_params=pltpu.CompilerParams(
            dimension_semantics=("arbitrary",), vmem_limit_bytes=16 << 20
        ),
        cost_estimate=pl.CostEstimate(
            flops=20 * explicit.size, bytes_accessed=8 * 10**6, transcendentals=0
        ),
    )(explicit, vertical, bottom, *got, *own)


def local(
    tracer,
    east_velocity,
    north_velocity,
    diffusivity,
    east_slope,
    north_slope,
    vertical_diffusivity,
    sea_mask,
    bottom,
):
    lon, lat = lax.axis_size("lon"), lax.axis_size("lat")
    args = (tracer, east_velocity, north_velocity, diffusivity, east_slope, north_slope, bottom)
    pay_a, pay_b, pay_c, pay_d, *own = pack(*args)

    def swap(pairs):
        return [p for a, b in pairs for p in ((a, b), (b, a))]

    def at(i, j):
        return i * lat + j

    near_lat = swap([(j, j + 1) for j in range(0, lat, 2)])
    far_lat = swap([(at(i, j), at(i, j + 1)) for i in range(lon) for j in range(1, lat - 1, 2)])
    far_lat += [(at(i, lat - 1), at(lon - 1 - i, lat - 1)) for i in range(lon)]
    near_lon = swap([(i, i + 1) for i in range(0, lon, 2)])
    far_lon = swap([(i, (i + 1) % lon) for i in range(1, lon, 2)])
    got_a = lax.ppermute(pay_a, "lat", near_lat)
    got_c = lax.ppermute(pay_c, "lon", near_lon)
    got_b = lax.ppermute(pay_b, ("lon", "lat"), far_lat)
    got_d = lax.ppermute(pay_d, "lon", far_lon)
    explicit = interior(*args)
    return solve(
        explicit, vertical_diffusivity, bottom, (got_a, got_b, got_c, got_d), tuple(own)
    )


def solution(mesh):
    field = P(None, "lat", "lon")
    placed = (
        P(None, None, "lat", "lon"),
        field,
        field,
        field,
        field,
        field,
        field,
        field,
        P("lat", "lon"),
    )
    return jax.shard_map(
        local, mesh=mesh, in_specs=placed, out_specs=P(None, None, "lat", "lon"), check_vma=False
    )
```

```python
import jax
import jax.numpy as jnp
from jax import lax
from jax.experimental import pallas as pl
from jax.experimental.pallas import tpu as pltpu
from jax.sharding import PartitionSpec as P

F32 = jnp.float32
LANES = 128
ROWS = 8
VMEM_LIMIT = 61 << 20
SOLVE_LIMIT = 32 << 20


def iota(shape, dim):
    return lax.broadcasted_iota(jnp.int32, shape, dim)


def minmod(first, second):
    return jnp.minimum(
        jnp.maximum(second, jnp.minimum(first, 0.0)), jnp.maximum(first, 0.0)
    )


def limiter_weight(speed):
    size = jnp.abs(speed)
    return 0.5 * size * (1.0 - size)


def pack_kernel(levels, tracers, rows, cols, lon_name, lat_name, *refs):
    (
        tracer_hbm,
        east_vel_hbm,
        north_vel_hbm,
        diff_hbm,
        east_slope_hbm,
        north_slope_hbm,
        bottom_hbm,
        pay_a,
        pay_b,
        pay_c,
        pay_d,
        own_lon,
        own_lat,
        own_lat_coef,
        tracer_v,
        east_vel_v,
        diff_v,
        east_slope_v,
        north_v,
        bottom_v,
        sems,
        row_sems,
    ) = refs
    items = levels * tracers
    group = 3
    groups = levels // group
    last = rows - ROWS
    copies = []
    row_copies = [pltpu.make_async_copy(bottom_hbm, bottom_v, row_sems.at[0])]
    for n, (src, start) in enumerate(
        ((north_vel_hbm, 0), (north_vel_hbm, last), (north_slope_hbm, 0), (north_slope_hbm, last))
    ):
        row_copies.append(
            pltpu.make_async_copy(
                src.at[:, pl.ds(start, ROWS), :], north_v.at[n], row_sems.at[n + 1]
            )
        )
    for g in range(groups):
        span = pl.ds(g * group, group)
        fetch = [
            pltpu.make_async_copy(
                tracer_hbm.at[:, span], tracer_v.at[:, span], sems.at[g, 0]
            )
        ]
        for n, (src, dst) in enumerate(
            ((diff_hbm, diff_v), (east_vel_hbm, east_vel_v), (east_slope_hbm, east_slope_v))
        ):
            fetch.append(pltpu.make_async_copy(src.at[span], dst.at[span], sems.at[g, n + 1]))
        copies.append(fetch)
    for copy in copies[0]:
        copy.start()
    for copy in row_copies:
        copy.start()
    for fetch in copies[1:]:
        for copy in fetch:
            copy.start()

    lane = iota((rows, LANES), 1)
    couple = lane // 2
    even = lane % 2 == 0
    left_side = lane < 64
    sub = iota((ROWS, cols), 0)
    right = cols - LANES
    zero = jnp.zeros((rows, LANES), F32)
    first_two = second = third_last = last_two = zero
    coefs = [[zero, zero] for _ in range(3)]
    row_at = (0, 1, 2, rows - 3, rows - 2, rows - 1)
    for copy in row_copies:
        copy.wait()
    row_bottoms = [bottom_v[r : r + 1, :] for r in row_at]
    block = [[jnp.zeros((ROWS, cols), F32)] * 6 for _ in range(items // ROWS)]
    edge_bottom = jnp.where(left_side, bottom_v[:, :LANES], bottom_v[:, right:])

    def turn(x, by):
        by = by % LANES
        return pltpu.roll(x, by, axis=1) if by else x

    for g in range(groups):
        for copy in copies[g]:
            copy.wait()
        for k in range(g * group, (g + 1) * group):
            sea = edge_bottom > k
            for t in range(tracers):
                n = k * tracers + t
                both = jnp.where(
                    left_side, tracer_v[t, k, :, :LANES], tracer_v[t, k, :, right:]
                )
                turned = turn(jnp.where(sea, both, 0.0), 2 * n)
                first_two = jnp.where(couple == n, turned, first_two)
                last_two = jnp.where(couple == (n - 1) % 64, turned, last_two)
                second = jnp.where(lane == 2 * n + 2, turned, second)
                third_last = jnp.where(lane == (2 * n - 3) % LANES, turned, third_last)
                for c, r in enumerate(row_at):
                    block[n // ROWS][c] = jnp.where(
                        sub == n % ROWS,
                        jnp.broadcast_to(tracer_v[t, k, r : r + 1, :], (ROWS, cols)),
                        block[n // ROWS][c],
                    )
            n = k * tracers
            for ref, outs in zip((diff_v, east_vel_v, east_slope_v), coefs):
                turned = turn(jnp.where(left_side, ref[k, :, :LANES], ref[k, :, right:]), 2 * n)
                outs[0] = jnp.where(couple == n, turned, outs[0])
                outs[1] = jnp.where(couple == (n - 1) % 64, turned, outs[1])
    cells = [
        first_two, turn(first_two, -1), turn(second, -2),
        turn(third_last, 3), turn(last_two, 2), turn(last_two, 1),
    ]
    head = lane % (2 * tracers) == 0

    def spread(x, by):
        x = jnp.where(head, turn(x, by), 0.0)
        x = x + turn(x, 2)
        return x + turn(x, 4)

    d_cols = [spread(coefs[0][i], by) for i, by in ((0, 0), (0, -1), (1, 2), (1, 1))]
    v_cols, s_cols = (
        [spread(pair[i], by) for i, by in ((0, 0), (1, 2), (1, 1))] for pair in coefs[1:]
    )
    level_of = couple // tracers
    inside = couple < items

    def column_mask(c):
        col = bottom_v[:, c : c + 1] if c >= 0 else bottom_v[:, cols + c : cols + c + 1]
        ok = (level_of < jnp.broadcast_to(col, (rows, LANES))) & inside
        return jnp.where(ok, 1.0, 0.0)

    m = [column_mask(c) for c in (0, 1, 2, -3, -2, -1)]
    jump_01 = (cells[1] - cells[0]) * (m[0] * m[1])
    jump_12 = (cells[2] - cells[1]) * (m[1] * m[2])
    jump_e0 = (cells[4] - cells[3]) * (m[3] * m[4])
    jump_e1 = (cells[5] - cells[4]) * (m[4] * m[5])

    def pair(low, high):
        return jnp.where(even, low, turn(high, 1))

    odd_lon = lax.rem(lax.axis_index(lon_name), 2) == 1
    odd_lat = lax.rem(lax.axis_index(lat_name), 2) == 1
    east = (pair(cells[5], jump_e1), pair(d_cols[3], v_cols[2]), pair(s_cols[2], m[5]))
    west = (pair(cells[0], jump_01), d_cols[0], pair(zero, m[0]))
    for n in range(3):
        pay_c[n] = jnp.where(odd_lon, west[n], east[n])
        pay_d[n] = jnp.where(odd_lon, east[n], west[n])
    for n, x in enumerate(
        [cells[0], cells[1], jump_12, cells[4], cells[5], jump_e0] + d_cols + v_cols + s_cols
    ):
        own_lon[n] = x

    for b in range(items // ROWS):
        at = pl.ds(b * ROWS, ROWS)
        level = (sub + b * ROWS) // tracers
        m = [
            jnp.where(level < jnp.broadcast_to(x, (ROWS, cols)), 1.0, 0.0) for x in row_bottoms
        ]
        x = [y * z for y, z in zip(block[b], m)]
        j01 = (x[1] - x[0]) * (m[0] * m[1])
        j12 = (x[2] - x[1]) * (m[1] * m[2])
        k0 = (x[4] - x[3]) * (m[3] * m[4])
        k1 = (x[5] - x[4]) * (m[4] * m[5])
        for n, y in enumerate((x[0], x[1], j12, x[4], x[5], k0)):
            own_lat[n, at, :] = y
        pay_a[at, :] = jnp.where(odd_lat, x[0], x[5])
        pay_b[at, :] = jnp.where(odd_lat, x[5], x[0])
        at = pl.ds(items + b * ROWS, ROWS)
        pay_a[at, :] = jnp.where(odd_lat, j01, k1)
        pay_b[at, :] = jnp.where(odd_lat, k1, j01)
    base = 2 * items
    for k in range(levels):
        values = (
            diff_v[k, 0:1, :],
            diff_v[k, 1:2, :],
            diff_v[k, rows - 2 : rows - 1, :],
            diff_v[k, rows - 1 : rows, :],
            north_v[0, k, 0:1, :],
            north_v[1, k, 6:7, :],
            north_v[1, k, 7:8, :],
            north_v[2, k, 0:1, :],
            north_v[3, k, 6:7, :],
            north_v[3, k, 7:8, :],
        )
        for n, y in enumerate(values):
            own_lat_coef[n, k : k + 1, :] = y
        for n, top in enumerate((values[3], values[6], values[9])):
            low = values[0] if n == 0 else jnp.zeros_like(top)
            r = base + n * levels + k
            pay_a[r : r + 1, :] = jnp.where(odd_lat, low, top)
            pay_b[r : r + 1, :] = jnp.where(odd_lat, top, low)
    r = base + 3 * levels
    low, top = row_bottoms[0].astype(F32), row_bottoms[5].astype(F32)
    pay_a[r : r + 1, :] = jnp.where(odd_lat, low, top)
    pay_b[r : r + 1, :] = jnp.where(odd_lat, top, low)
    for q in range(r + 1, pay_a.shape[0]):
        pay_a[q : q + 1, :] = jnp.zeros_like(low)
        pay_b[q : q + 1, :] = jnp.zeros_like(low)


def pack(tracer, east_vel, north_vel, diff, east_slope, north_slope, bottom):
    tracers, levels, rows, cols = tracer.shape
    items = tracers * levels
    lat_rows = -(-(2 * items + 3 * levels + 1) // ROWS) * ROWS
    shape = jax.ShapeDtypeStruct
    vmem = pl.BlockSpec(memory_space=pltpu.VMEM)

    def body(*refs):
        pack_kernel(levels, tracers, rows, cols, "lon", "lat", *refs)

    return pl.pallas_call(
        body,
        name="pack_edges",
        in_specs=[pl.BlockSpec(memory_space=pltpu.HBM)] * 7,
        out_specs=[vmem] * 7,
        out_shape=[
            shape((lat_rows, cols), F32),
            shape((lat_rows, cols), F32),
            shape((3, rows, LANES), F32),
            shape((3, rows, LANES), F32),
            shape((16, rows, LANES), F32),
            shape((6, items, cols), F32),
            shape((10, levels, cols), F32),
        ],
        scratch_shapes=[
            pltpu.VMEM((tracers, levels, rows, cols), F32),
            pltpu.VMEM((levels, rows, cols), F32),
            pltpu.VMEM((levels, rows, cols), F32),
            pltpu.VMEM((levels, rows, cols), F32),
            pltpu.VMEM((4, levels, ROWS, cols), F32),
            pltpu.VMEM((rows, cols), jnp.int32),
            pltpu.SemaphoreType.DMA((levels // 3, 4)),
            pltpu.SemaphoreType.DMA((5,)),
        ],
        compiler_params=pltpu.CompilerParams(vmem_limit_bytes=VMEM_LIMIT),
        cost_estimate=pl.CostEstimate(flops=10**6, bytes_accessed=7 * 10**6, transcendentals=0),
    )(tracer, east_vel, north_vel, diff, east_slope, north_slope, bottom)


def interior_kernel(levels, tracers, rows, cols, span, *refs):
    sources = refs[:6]
    bottom_hbm, explicit_hbm = refs[6], refs[-23]
    (
        tracer,
        east_vel,
        north_vel,
        diff,
        east_slope,
        north_slope,
        bottom,
        explicit,
        sems,
        bottom_sem,
        out_sems,
        ring,
        ring_sum,
        step_here,
        step_west,
        bend_here,
        bend_east,
        flux_west,
        partial,
        north_part,
        open_at,
        coef,
    ) = refs[-22:]
    first, stop = span()
    blocks = rows // ROWS
    halves = (slice(0, LANES), slice(LANES, 2 * LANES))
    lane = iota((ROWS, LANES), 1)
    sub = iota((ROWS, LANES), 0)

    def chunk(b):
        return slice(b * ROWS, (b + 1) * ROWS)

    def east_of(x):
        left, right = x
        turned = pltpu.roll(right, LANES - 1, axis=1)
        return (
            jnp.where(lane == LANES - 1, turned, pltpu.roll(left, LANES - 1, axis=1)),
            turned,
        )

    def west_of(x):
        left, right = x
        turned = pltpu.roll(left, 1, axis=1)
        return turned, jnp.where(lane == 0, turned, pltpu.roll(right, 1, axis=1))

    def up(x):
        return tuple(pltpu.roll(y, ROWS - 1, axis=0) for y in x)

    def down(x):
        return tuple(pltpu.roll(y, 1, axis=0) for y in x)

    def north_of(turned, turned_next):
        if turned_next is None:
            return turned
        return tuple(jnp.where(sub == ROWS - 1, n, y) for y, n in zip(turned, turned_next))

    def south_of(turned, turned_before):
        if turned_before is None:
            return turned
        return tuple(jnp.where(sub == 0, n, y) for y, n in zip(turned, turned_before))

    def load(ref, *index):
        *lead, b = index
        return tuple(ref[(*lead, chunk(b), h)] for h in halves)

    def save(ref, values, *index):
        *lead, b = index
        for h, x in zip(halves, values):
            ref[(*lead, chunk(b), h)] = x

    def sub2(x, y):
        return tuple(p - q for p, q in zip(x, y))

    def add2(x, y):
        return tuple(p + q for p, q in zip(x, y))

    def low2(x, y):
        return tuple(jnp.minimum(p, q) for p, q in zip(x, y))

    units = [(t, b) for b in range(blocks) for t in range(tracers)]

    def fetch(n, level):
        src, dst = sources[n], (tracer, east_vel, north_vel, diff, east_slope, north_slope)[n]
        if n == 0:
            src, dst = src.at[:, level], dst.at[:, level]
        else:
            src, dst = src.at[level], dst.at[level]
        return pltpu.make_async_copy(src, dst, sems.at[n, level])

    def store(level):
        return pltpu.make_async_copy(
            explicit.at[:, level], explicit_hbm.at[:, level], out_sems.at[level]
        )

    def each_level(low, high, body):
        def run(level, carry):
            body(level)
            return carry

        lax.fori_loop(low, high, run, 0)

    def take_in(level, slot, out):
        at = jnp.clip(level, 0, levels - 1)
        depth = jnp.where(level < 0, levels, level)
        for b in range(blocks):
            sea = tuple(x > depth for x in load(bottom, b))
            for t in range(tracers):
                here = tuple(
                    jnp.where(s, x, 0.0) for s, x in zip(sea, load(tracer, t, at, b))
                )
                east = east_of(here)
                save(ring, here, slot, t, b)
                save(ring_sum, add2(here, east), slot, t, b)
                save(step_here, sub2(east, here), out, t, b)

    def take_steps(out):
        for t, b in units:
            save(step_west, west_of(load(step_here, out, t, b)), out, t, b)

    before_first = jnp.maximum(first - 1, 0)
    past_last = jnp.minimum(stop + 1, levels)
    started = first < stop

    @pl.when(started)
    def _():
        at_bottom = pltpu.make_async_copy(bottom_hbm, bottom, bottom_sem)
        at_bottom.start()

        def begin(level):
            fetch(0, level).start()

            @pl.when((level >= first) & (level < stop))
            def _():
                for n in range(1, 6):
                    fetch(n, level).start()

        each_level(before_first, past_last, begin)
        at_bottom.wait()
        depth = [load(bottom, b) for b in range(blocks)]
        ups, downs = [up(x) for x in depth], [down(x) for x in depth]
        east = [low2(x, east_of(x)) for x in depth]
        east_both = [low2(x, west_of(x)) for x in east]
        north = [
            low2(x, north_of(ups[b], ups[b + 1] if b + 1 < blocks else None))
            for b, x in enumerate(depth)
        ]
        north_downs = [down(x) for x in north]
        north_both = [
            low2(x, south_of(north_downs[b], north_downs[b - 1] if b else None))
            for b, x in enumerate(north)
        ]
        north_ups = [up(x) for x in north_both]
        for b in range(blocks):
            row = sub + b * ROWS
            inner_rows = (row > 0) & (row < rows - 2)
            inner = tuple(
                (lane + i * LANES > 0) & (lane + i * LANES < cols - 2) for i in range(2)
            )
            save(open_at, tuple(jnp.where(c, x, 0) for c, x in zip(inner, east[b])), 0, b)
            save(open_at, east_both[b], 1, b)
            save(open_at, east_of(east_both[b]), 2, b)
            save(open_at, tuple(jnp.where(inner_rows, x, 0) for x in north[b]), 3, b)
            save(open_at, north_both[b], 4, b)
            save(
                open_at,
                north_of(north_ups[b], north_ups[b + 1] if b + 1 < blocks else None),
                5,
                b,
            )
        @pl.when(first > 0)
        def _():
            fetch(0, first - 1).wait()

        fetch(0, first).wait()
        take_in(first - 1, lax.rem(first + 2, 3), lax.rem(first + 1, 2))
        take_in(first, lax.rem(first, 3), lax.rem(first, 2))
        take_steps(lax.rem(first, 2))

    def one_level(level):
        now, later, before = lax.rem(level, 3), lax.rem(level + 1, 3), lax.rem(level + 2, 3)
        nth = lax.rem(level, 2)
        nth_next = 1 - nth
        for n in range(1, 6):
            fetch(n, level).wait()

        @pl.when(level + 1 < levels)
        def _():
            fetch(0, level + 1).wait()

        for t, b in units:
            bend = tuple(
                minmod(x, y)
                for x, y in zip(load(step_here, nth, t, b), load(step_west, nth, t, b))
            )
            save(bend_here, bend, t, b)
            save(bend_east, east_of(bend), t, b)

        take_in(level + 1, later, nth_next)

        for b in range(blocks):
            here = load(diff, level, b)
            north = north_of(up(here), up(load(diff, level, min(b + 1, blocks - 1))))
            for way, other, vel, slope in (
                (0, east_of(here), east_vel, east_slope),
                (1, north, north_vel, north_slope),
            ):
                for i, h in enumerate(halves):
                    at = (chunk(b), h)
                    face = open_at[(3 * way, *at)] > level
                    speed = jnp.where(face, vel[(level, *at)], 0.0)
                    mean = jnp.where(face, 0.5 * (here[i] + other[i]), 0.0)
                    depth = jnp.where(
                        speed >= 0, open_at[(3 * way + 1, *at)], open_at[(3 * way + 2, *at)]
                    )
                    coef[(4 * way, *at)] = speed
                    coef[(4 * way + 1, *at)] = jnp.where(depth > level, limiter_weight(speed), 0.0)
                    coef[(4 * way + 2, *at)] = mean - jnp.minimum(speed, 0.0)
                    coef[(4 * way + 3, *at)] = 0.125 * slope[(level, *at)] * mean

        def face(way, b, here, step, bend, bend_other, tilt):
            out = []
            for i, h in enumerate(halves):
                at = (chunk(b), h)
                speed = coef[(4 * way, *at)]
                limited = jnp.where(speed >= 0, bend[i], bend_other[i])
                out.append(
                    (coef[(4 * way + 2, *at)] * step[i] - coef[(4 * way + 3, *at)] * tilt[i])
                    - (speed * here[i] + coef[(4 * way + 1, *at)] * limited)
                )
            return tuple(out)

        def north_faces(t):
            def stage(b):
                here = load(ring, now, t, b)
                tilt = sub2(load(ring, later, t, b), load(ring, before, t, b))
                return here, up(here), tilt, up(tilt)

            this = stage(0)
            step_before = flux_before = held = None
            for b in range(blocks + 1):
                if b < blocks:
                    nxt = stage(b + 1) if b + 1 < blocks else (None,) * 4
                    here, turned, tilt, tilt_turned = this
                    north = north_of(turned, nxt[1])
                    step = sub2(north, here)
                    step_turned = down(step)
                    bend = tuple(
                        minmod(x, y) for x, y in zip(step, south_of(step_turned, step_before))
                    )
                    bend_turned = up(bend)
                    step_before = step_turned
                if held is not None:
                    pb, p_here, p_step, p_bend, p_bend_turned, p_tilt = held
                    bend_n = north_of(p_bend_turned, bend_turned if b < blocks else None)
                    flux = face(1, pb, p_here, p_step, p_bend, bend_n, p_tilt)
                    flux_turned = down(flux)
                    if flux_before is None:
                        flux_s = tuple(jnp.where(sub == 0, 0.0, y) for y in flux_turned)
                    else:
                        flux_s = south_of(flux_turned, flux_before)
                    flux_before = flux_turned
                    save(north_part, add2(p_here, sub2(flux, flux_s)), t, pb)
                if b < blocks:
                    held = (
                        b, here, step, bend, bend_turned,
                        add2(tilt, north_of(tilt_turned, nxt[3])),
                    )
                    this = nxt

        for t in range(0, tracers, 2):
            north_faces(t)

        for t, b in units:
            flux = face(
                0,
                b,
                load(ring, now, t, b),
                load(step_here, nth, t, b),
                load(bend_here, t, b),
                load(bend_east, t, b),
                sub2(load(ring_sum, later, t, b), load(ring_sum, before, t, b)),
            )
            left, right = west_of(flux)
            save(flux_west, (jnp.where(lane == 0, 0.0, left), right), t, b)
            save(partial, flux, t, b)

        take_steps(nth_next)

        for t in range(1, tracers, 2):
            north_faces(t)

        for t, b in units:
            total = add2(
                load(north_part, t, b), sub2(load(partial, t, b), load(flux_west, t, b))
            )
            save(explicit, total, t, level, b)

        store(level).start()

    each_level(first, stop, one_level)
    each_level(first, stop, lambda level: store(level).wait())


def interior(tracer, east_vel, north_vel, diff, east_slope, north_slope, bottom, span, so_far=None):
    tracers, levels, rows, cols = tracer.shape

    def body(*refs):
        interior_kernel(levels, tracers, rows, cols, span, *refs)

    plane = (tracers, rows, cols)
    field = pltpu.VMEM((levels, rows, cols), F32)
    args = (tracer, east_vel, north_vel, diff, east_slope, north_slope, bottom)
    args = args if so_far is None else (*args, so_far)
    hbm = pl.BlockSpec(memory_space=pltpu.HBM)
    return pl.pallas_call(
        body,
        name="interior_faces",
        in_specs=[hbm] * len(args),
        out_specs=hbm,
        out_shape=jax.ShapeDtypeStruct(tracer.shape, F32),
        input_output_aliases={} if so_far is None else {7: 0},
        scratch_shapes=[
            pltpu.VMEM(tracer.shape, F32),
            field,
            field,
            field,
            field,
            field,
            pltpu.VMEM((rows, cols), jnp.int32),
            pltpu.VMEM(tracer.shape, F32),
            pltpu.SemaphoreType.DMA((6, levels)),
            pltpu.SemaphoreType.DMA,
            pltpu.SemaphoreType.DMA((levels,)),
            pltpu.VMEM((3, *plane), F32),
            pltpu.VMEM((3, *plane), F32),
            pltpu.VMEM((2, *plane), F32),
            pltpu.VMEM((2, *plane), F32),
            pltpu.VMEM(plane, F32),
            pltpu.VMEM(plane, F32),
            pltpu.VMEM(plane, F32),
            pltpu.VMEM(plane, F32),
            pltpu.VMEM(plane, F32),
            pltpu.VMEM((6, rows, cols), jnp.int32),
            pltpu.VMEM((8, rows, cols), F32),
        ],
        compiler_params=pltpu.CompilerParams(vmem_limit_bytes=VMEM_LIMIT),
        cost_estimate=pl.CostEstimate(
            flops=60 * tracer.size, bytes_accessed=12 * 10**6, transcendentals=0
        ),
    )(*args)


def edge_faces(m1, m2, m3, j0, j3, open1, open2, d1, d2, d3, v0, v1, s0, s1, tilt):
    j1 = (m2 - m1) * open1
    j2 = (m3 - m2) * open2
    t1, t2, t3 = tilt(m1), tilt(m2), tilt(m3)

    def face(low, high, behind, jump, ahead, opened, d_sum, vel, slope, tilts):
        speed = vel * opened
        forward = speed >= 0
        flux = speed * jnp.where(forward, low, high) + limiter_weight(speed) * minmod(
            jump, jnp.where(forward, behind, ahead)
        )
        return 0.5 * d_sum * (jump - 0.125 * slope * opened * tilts) - flux

    return (
        face(m1, m2, j0, j1, j2, open1, d1 + d2, v0, s0, t1 + t2),
        face(m2, m3, j1, j2, j3, open2, d2 + d3, v1, s1, t2 + t3),
    )


def solve_kernel(levels, tracers, rows, cols, lon_name, lat_name, lat_count, *refs):
    (
        explicit_hbm,
        vertical_hbm,
        bottom,
        got_a,
        got_b,
        got_c,
        got_d,
        own_lon,
        own_lat,
        own_lat_coef,
        out_hbm,
        field,
        vertical,
        fix_lon,
        fix_lat,
        south,
        north,
        pivots,
        in_sems,
        out_sems,
    ) = refs
    blocks = rows // ROWS
    items = levels * tracers
    base = 2 * items
    halves = (slice(0, LANES), slice(LANES, 2 * LANES))
    lane = iota((ROWS, LANES), 1)
    sub = iota((ROWS, LANES), 0)

    def rows_of(b):
        if isinstance(b, int):
            return pl.ds(b * ROWS, ROWS)
        return pl.ds(pl.multiple_of(b * ROWS, ROWS), ROWS)

    def fetch(b):
        at = rows_of(b)
        return (
            pltpu.make_async_copy(
                explicit_hbm.at[:, :, at, :], field.at[:, :, at, :], in_sems.at[0, b]
            ),
            pltpu.make_async_copy(
                vertical_hbm.at[:, at, :], vertical.at[:, at, :], in_sems.at[1, b]
            ),
        )

    def store(b):
        at = rows_of(b)
        return pltpu.make_async_copy(
            field.at[:, :, at, :], out_hbm.at[:, :, at, :], out_sems.at[b]
        )

    for b in range(blocks):
        for copy in fetch(b):
            copy.start()

    def edges():
        odd_lon = lax.rem(lax.axis_index(lon_name), 2) == 1
        lat = lax.axis_index(lat_name)
        odd_lat = lax.rem(lat, 2) == 1
        top = lat == lat_count - 1
        even = lane % 2 == 0
        inside = lane < 2 * items
        level = lane // (2 * tracers)

        def tilt_lanes(x):
            return pltpu.roll(x, LANES - 2 * tracers, axis=1) - pltpu.roll(
                x, 2 * tracers, axis=1
            )

        for b in range(blocks):
            at = slice(b * ROWS, (b + 1) * ROWS)

            def mask(c):
                col = jnp.broadcast_to(bottom[at, c : c + 1], (ROWS, LANES))
                return jnp.where((level < col) & inside, 1.0, 0.0)

            def halves_of(pays):
                return pays, [pltpu.roll(x, LANES - 1, axis=1) for x in pays]

            c_got = [got_c[n, at, :] for n in range(3)]
            d_got = [got_d[n, at, :] for n in range(3)]
            from_west = [jnp.where(odd_lon, c, d) for c, d in zip(c_got, d_got)]
            from_east = [jnp.where(odd_lon, d, c) for c, d in zip(c_got, d_got)]
            own = [own_lon[n, at, :] for n in range(16)]
            (wm, wd, ws), (wj, wv, wk) = halves_of(from_west)
            m0, m1 = mask(0), mask(1)
            f0, f1 = edge_faces(
                wm, own[0], own[1], wj, own[2], wk * m0, m0 * m1,
                wd, own[6], own[7], wv, own[10], ws, own[13], tilt_lanes,
            )
            fix_lon[0, at, :] = jnp.where(
                even, (f1 - f0) * m0, pltpu.roll(-f1 * m1, 1, axis=1)
            )
            (em, ed, _), (ej, _, ek) = halves_of(from_east)
            m0, m1 = mask(cols - 2), mask(cols - 1)
            f0, f1 = edge_faces(
                own[3], own[4], em, own[5], ej, m0 * m1, m1 * ek,
                own[8], own[9], ed, own[11], own[12], own[14], own[15], tilt_lanes,
            )
            fix_lon[1, at, :] = jnp.where(
                even, f0 * m0, pltpu.roll((f1 - f0) * m1, 1, axis=1)
            )

        south[...] = jnp.where(odd_lat, got_a[...], got_b[...])

        @pl.when(jnp.logical_not(top))
        def _():
            north[...] = jnp.where(odd_lat, got_b[...], got_a[...])

        @pl.when(top)
        def _():
            mirror = LANES - 1 - lane
            for b in range(north.shape[0] // ROWS):
                at = slice(b * ROWS, (b + 1) * ROWS)
                for i in range(2):
                    north[at, halves[i]] = jnp.take_along_axis(
                        got_b[at, halves[1 - i]], mirror, axis=1, mode="promise_in_bounds"
                    )

        wide = iota((ROWS, cols), 0)
        sign = jnp.where(top, -1.0, 1.0)

        def spread_rows(ref, first, b):
            k = b * ROWS // tracers
            low, high = ref[first + k : first + k + 1, :], ref[first + k + 1 : first + k + 2, :]
            return jnp.where(
                wide < tracers,
                jnp.broadcast_to(low, (ROWS, cols)),
                jnp.broadcast_to(high, (ROWS, cols)),
            )

        def tilt_rows_of(read):
            def tilt(b):
                here = read(b)
                zeros = jnp.zeros_like(here)
                turned = pltpu.roll(here, tracers, axis=0)
                after = pltpu.roll(read(b + 1), tracers, axis=0) if b + 1 < items // ROWS else zeros
                before = pltpu.roll(read(b - 1), tracers, axis=0) if b else zeros
                return jnp.where(wide < tracers, turned, after) - jnp.where(
                    wide < tracers, before, turned
                )

            return tilt

        def own_row(n):
            return lambda b: own_lat[n, b * ROWS : (b + 1) * ROWS, :]

        def ghost_row(ref):
            return lambda b: ref[b * ROWS : (b + 1) * ROWS, :]

        for b in range(items // ROWS):
            at = slice(b * ROWS, (b + 1) * ROWS)
            past = slice(items + b * ROWS, items + (b + 1) * ROWS)
            level = (wide + b * ROWS) // tracers

            def mask(row):
                return jnp.where(level < jnp.broadcast_to(row, (ROWS, cols)), 1.0, 0.0)

            def coef(n):
                return spread_rows(own_lat_coef.at[n], 0, b)

            def ghost_mask(ref):
                row = ref[base + 3 * levels : base + 3 * levels + 1, :]
                return jnp.where(level.astype(F32) < jnp.broadcast_to(row, (ROWS, cols)), 1.0, 0.0)

            south_mask = jnp.where(lat > 0, ghost_mask(south), 0.0)

            def run(reads, j0, j3, open1, open2, d, v, s):
                tilts = [tilt_rows_of(r)(b) for r in reads]
                values = [r(b) for r in reads]
                lookup = dict(zip(map(id, values), tilts))
                return edge_faces(*values, j0, j3, open1, open2, *d, *v, *s,
                                  lambda x: lookup[id(x)])

            m0, m1 = mask(bottom[0:1, :]), mask(bottom[1:2, :])
            f0, f1 = run(
                (ghost_row(south), own_row(0), own_row(1)),
                jnp.where(lat > 0, south[past, :], 0.0), own_lat[2, at, :], south_mask * m0, m0 * m1,
                (spread_rows(south, base, b), coef(0), coef(1)),
                (spread_rows(south, base + levels, b), coef(4)),
                (spread_rows(south, base + 2 * levels, b), coef(7)),
            )
            fix_lat[0, at, :] = (f1 - f0) * m0
            fix_lat[1, at, :] = -f1 * m1
            m0 = mask(bottom[rows - 2 : rows - 1, :])
            m1 = mask(bottom[rows - 1 : rows, :])
            top_vel = coef(6)
            ghost_vel = spread_rows(north, base + levels, b)
            top_vel = jnp.where(top, 0.5 * (top_vel - ghost_vel), top_vel)
            f0, f1 = run(
                (own_row(3), own_row(4), ghost_row(north)),
                own_lat[5, at, :], sign * north[past, :], m0 * m1, m1 * ghost_mask(north),
                (coef(2), coef(3), spread_rows(north, base, b)),
                (coef(5), top_vel),
                (coef(8), coef(9)),
            )
            fix_lat[2, at, :] = f0 * m0
            fix_lat[3, at, :] = (f1 - f0) * m1

    edges()

    def one_block(step, carry):
        at = rows_of(step)
        for copy in fetch(step):
            copy.wait()
        first_block = step == 0
        row0 = jnp.where(first_block, 0, ROWS - 2)
        pick = jnp.where(first_block, 0, 2)

        @pl.when(first_block | (step == blocks - 1))
        def _():
            for t in range(tracers):
                for k in range(levels):
                    n = k * tracers + t
                    for h in halves:
                        low = jnp.broadcast_to(fix_lat[pick, n : n + 1, h], (ROWS, LANES))
                        high = jnp.broadcast_to(fix_lat[pick + 1, n : n + 1, h], (ROWS, LANES))
                        field[t, k, at, h] = field[t, k, at, h] + jnp.where(
                            sub == row0, low, jnp.where(sub == row0 + 1, high, 0.0)
                        )

        depth = tuple(bottom[at, h] for h in halves)
        for i, h in enumerate(halves):
            ratio = above = None
            for k in range(levels):
                if k + 1 < levels:
                    below = jnp.where(depth[i] > k + 1, vertical[k, at, h], 0.0)
                if k == 0:
                    pivot = 1.0 + below
                elif k + 1 < levels:
                    pivot = (1.0 + above + below) + above * ratio
                else:
                    pivot = (1.0 + above) + above * ratio
                inverse = 1.0 / pivot
                pivots[0, k, :, h] = inverse
                if k:
                    pivots[1, k, :, h] = above
                if k + 1 < levels:
                    ratio = below * inverse
                    pivots[2, k, :, h] = ratio
                    above = below

        fixes = [fix_lon[i, at, :] for i in range(2)]
        for t in range(tracers):
            for i, h in enumerate(halves):
                begin = 0 if i == 0 else LANES - 2
                near = lane < 2 if i == 0 else lane >= LANES - 2
                values = []
                value = None
                for k in range(levels):
                    turn = (begin - 2 * (k * tracers + t)) % LANES
                    patch = pltpu.roll(fixes[i], turn, axis=1) if turn else fixes[i]
                    right = field[t, k, at, h] + jnp.where(near, patch, 0.0)
                    right = jnp.where(depth[i] > k, right, 0.0)
                    if k:
                        right = right + pivots[1, k, :, h] * value
                    value = right * pivots[0, k, :, h]
                    values.append(value)
                nxt = values[-1]
                field[t, levels - 1, at, h] = nxt
                for k in range(levels - 2, -1, -1):
                    nxt = values[k] + pivots[2, k, :, h] * nxt
                    field[t, k, at, h] = nxt
        store(step).start()
        return carry

    lax.fori_loop(0, blocks, one_block, 0)
    for b in range(blocks):
        store(b).wait()


def solve(explicit, vertical, bottom, got, own):
    tracers, levels, rows, cols = explicit.shape
    items = levels * tracers
    lat_rows = got[0].shape[0]
    lat_count = lax.axis_size("lat")
    blocks = rows // ROWS

    def body(*refs):
        solve_kernel(levels, tracers, rows, cols, "lon", "lat", lat_count, *refs)

    hbm = pl.BlockSpec(memory_space=pltpu.HBM)
    vmem = pl.BlockSpec(memory_space=pltpu.VMEM)
    return pl.pallas_call(
        body,
        name="edges_and_solve",
        in_specs=[hbm, hbm] + [vmem] * 8,
        out_specs=hbm,
        out_shape=jax.ShapeDtypeStruct(explicit.shape, F32),
        input_output_aliases={0: 0},
        scratch_shapes=[
            pltpu.VMEM(explicit.shape, F32),
            pltpu.VMEM(vertical.shape, F32),
            pltpu.VMEM((2, rows, LANES), F32),
            pltpu.VMEM((4, items, cols), F32),
            pltpu.VMEM((lat_rows, cols), F32),
            pltpu.VMEM((lat_rows, cols), F32),
            pltpu.VMEM((3, levels, ROWS, cols), F32),
            pltpu.SemaphoreType.DMA((2, blocks)),
            pltpu.SemaphoreType.DMA((blocks,)),
        ],
        compiler_params=pltpu.CompilerParams(vmem_limit_bytes=SOLVE_LIMIT),
        cost_estimate=pl.CostEstimate(
            flops=20 * explicit.size, bytes_accessed=8 * 10**6, transcendentals=0
        ),
    )(explicit, vertical, bottom, *got, *own)


def local(
    tracer,
    east_velocity,
    north_velocity,
    diffusivity,
    east_slope,
    north_slope,
    vertical_diffusivity,
    sea_mask,
    bottom,
):
    lon, lat = lax.axis_size("lon"), lax.axis_size("lat")
    levels = tracer.shape[1]
    args = (tracer, east_velocity, north_velocity, diffusivity, east_slope, north_slope, bottom)
    pay_a, pay_b, pay_c, pay_d, *own = pack(*args)

    def swap(pairs):
        return [p for a, b in pairs for p in ((a, b), (b, a))]

    def at(i, j):
        return i * lat + j

    near_lat = swap([(j, j + 1) for j in range(0, lat, 2)])
    far_lat = swap([(at(i, j), at(i, j + 1)) for i in range(lon) for j in range(1, lat - 1, 2)])
    far_lat += [(at(i, lat - 1), at(lon - 1 - i, lat - 1)) for i in range(lon)]
    far_lat += swap([(at(i, 0), at(i + 1, 0)) for i in range(0, lon, 2)])
    near_lon = swap([(i, i + 1) for i in range(0, lon, 2)])
    far_lon = swap([(i, (i + 1) % lon) for i in range(1, lon, 2)])
    got_a = lax.ppermute(pay_a, "lat", near_lat)
    got_c = lax.ppermute(pay_c, "lon", near_lon)
    got_b = lax.ppermute(pay_b, ("lon", "lat"), far_lat)
    got_d = lax.ppermute(pay_d, "lon", far_lon)
    explicit = interior(*args, lambda: (0, levels))
    return solve(
        explicit, vertical_diffusivity, bottom, (got_a, got_b, got_c, got_d), tuple(own)
    )


def solution(mesh):
    field = P(None, "lat", "lon")
    placed = (
        P(None, None, "lat", "lon"),
        field,
        field,
        field,
        field,
        field,
        field,
        field,
        P("lat", "lon"),
    )
    return jax.shard_map(
        local, mesh=mesh, in_specs=placed, out_specs=P(None, None, "lat", "lon"), check_vma=False
    )
```

```python
import jax
import jax.numpy as jnp
from jax import lax
from jax.experimental import pallas as pl
from jax.experimental.pallas import tpu as pltpu
from jax.sharding import PartitionSpec as P

F32 = jnp.float32
LANES = 128
ROWS = 8
VMEM_LIMIT = 40 << 20
SOLVE_LIMIT = 32 << 20


def iota(shape, dim):
    return lax.broadcasted_iota(jnp.int32, shape, dim)


def minmod(first, second):
    return jnp.minimum(
        jnp.maximum(second, jnp.minimum(first, 0.0)), jnp.maximum(first, 0.0)
    )


def limiter_weight(speed):
    size = jnp.abs(speed)
    return 0.5 * size * (1.0 - size)


def pack_kernel(levels, tracers, rows, cols, lon_name, lat_name, *refs):
    sources = refs[:7]
    (
        pay_a,
        pay_b,
        pay_c,
        pay_d,
        own_lon,
        own_lat,
        own_lat_coef,
        tracer_v,
        east_vel_v,
        diff_v,
        east_slope_v,
        bottom_v,
        north_v,
        gathered,
        turned_v,
        sems,
        row_sems,
    ) = refs[7:]
    tracer_hbm, east_vel_hbm, north_vel_hbm, diff_hbm, east_slope_hbm, north_slope_hbm = sources[:6]
    items = levels * tracers
    group = ROWS // tracers
    groups = levels // group
    last = rows - ROWS
    right = cols - LANES
    base = 2 * items
    row_copies = [pltpu.make_async_copy(sources[6], bottom_v, row_sems.at[0])]
    for n, (src, start) in enumerate(
        ((north_vel_hbm, 0), (north_vel_hbm, last), (north_slope_hbm, 0), (north_slope_hbm, last))
    ):
        row_copies.append(
            pltpu.make_async_copy(
                src.at[:, pl.ds(start, ROWS), :], north_v.at[n], row_sems.at[n + 1]
            )
        )
    copies = []
    for g in range(groups):
        span = pl.ds(g * group, group)
        fetch = [
            pltpu.make_async_copy(
                tracer_hbm.at[:, span], tracer_v.at[:, span], sems.at[g, 0]
            )
        ]
        for n, (src, dst) in enumerate(
            ((diff_hbm, diff_v), (east_vel_hbm, east_vel_v), (east_slope_hbm, east_slope_v))
        ):
            fetch.append(pltpu.make_async_copy(src.at[span], dst.at[span], sems.at[g, n + 1]))
        copies.append(fetch)
    row_copies[0].start()
    for copy in copies[0]:
        copy.start()
    for copy in row_copies[1:]:
        copy.start()
    for fetch in copies[1:]:
        for copy in fetch:
            copy.start()

    lane = iota((ROWS, LANES), 1)
    couple = lane // 2
    even = lane % 2 == 0
    left_side = lane < 64
    sub = iota((ROWS, cols), 0)
    row_at = (0, 1, 2, rows - 3, rows - 2, rows - 1)
    odd_lon = lax.rem(lax.axis_index(lon_name), 2) == 1
    odd_lat = lax.rem(lax.axis_index(lat_name), 2) == 1
    chunks = [slice(r * ROWS, (r + 1) * ROWS) for r in range(rows // ROWS)]

    def turn(x, by):
        by = by % LANES
        return pltpu.roll(x, by, axis=1) if by else x

    def send_rows(at, low, top):
        pay_a[at, :] = jnp.where(odd_lat, low, top)
        pay_b[at, :] = jnp.where(odd_lat, top, low)

    row_copies[0].wait()
    row_bottoms = [bottom_v[r : r + 1, :] for r in row_at]
    for g in range(groups):
        for copy in copies[g]:
            copy.wait()
        for k in range(g * group, (g + 1) * group):
            j = (k - g * group) * (tracers + 3)
            for at in chunks:
                sea = jnp.where(left_side, bottom_v[at, :LANES], bottom_v[at, right:]) > k
                for t in range(tracers):
                    both = jnp.where(
                        left_side, tracer_v[t, k, at, :LANES], tracer_v[t, k, at, right:]
                    )
                    turned_v[j + t, at, :] = turn(
                        jnp.where(sea, both, 0.0), 2 * (k * tracers + t)
                    )
                for i, ref in enumerate((diff_v, east_vel_v, east_slope_v)):
                    both = jnp.where(left_side, ref[k, at, :LANES], ref[k, at, right:])
                    turned_v[j + tracers + i, at, :] = turn(both, 2 * k * tracers)
        first = g * group
        x = []
        m = []
        level = sub // tracers + first
        for c, r in enumerate(row_at):
            rows_in = jnp.broadcast_to(tracer_v[0, first, r : r + 1, :], (ROWS, cols))
            for q in range(1, ROWS):
                row = tracer_v[q % tracers, first + q // tracers, r : r + 1, :]
                rows_in = jnp.where(sub == q, jnp.broadcast_to(row, (ROWS, cols)), rows_in)
            m.append(
                jnp.where(level < jnp.broadcast_to(row_bottoms[c], (ROWS, cols)), 1.0, 0.0)
            )
            x.append(rows_in * m[c])
        at = pl.ds(g * ROWS, ROWS)
        for n, y in enumerate(
            (
                x[0],
                x[1],
                (x[2] - x[1]) * (m[1] * m[2]),
                x[4],
                x[5],
                (x[4] - x[3]) * (m[3] * m[4]),
            )
        ):
            own_lat[n, at, :] = y
        send_rows(at, x[0], x[5])
        send_rows(
            pl.ds(items + g * ROWS, ROWS),
            (x[1] - x[0]) * (m[0] * m[1]),
            (x[5] - x[4]) * (m[4] * m[5]),
        )
        if g == 0:
            for copy in row_copies[1:]:
                copy.wait()
        for k in range(first, first + group):
            values = (
                diff_v[k, 0:1, :],
                diff_v[k, 1:2, :],
                diff_v[k, rows - 2 : rows - 1, :],
                diff_v[k, rows - 1 : rows, :],
                north_v[0, k, 0:1, :],
                north_v[1, k, 6:7, :],
                north_v[1, k, 7:8, :],
                north_v[2, k, 0:1, :],
                north_v[3, k, 6:7, :],
                north_v[3, k, 7:8, :],
            )
            for n, y in enumerate(values):
                own_lat_coef[n, k : k + 1, :] = y
            for n, top in enumerate((values[3], values[6], values[9])):
                low = values[0] if n == 0 else jnp.zeros_like(top)
                r = base + n * levels + k
                send_rows(slice(r, r + 1), low, top)
        for at in chunks:
            acc = [gathered[n, at, :] if g else jnp.zeros((ROWS, LANES), F32) for n in range(10)]
            for k in range(first, first + group):
                j = (k - first) * (tracers + 3)
                for t in range(tracers):
                    n = k * tracers + t
                    turned = turned_v[j + t, at, :]
                    acc[0] = jnp.where(couple == n, turned, acc[0])
                    acc[1] = jnp.where(couple == (n - 1) % 64, turned, acc[1])
                    acc[2] = jnp.where(lane == 2 * n + 2, turned, acc[2])
                    acc[3] = jnp.where(lane == (2 * n - 3) % LANES, turned, acc[3])
                n = k * tracers
                for i in range(3):
                    turned = turned_v[j + tracers + i, at, :]
                    acc[4 + 2 * i] = jnp.where(couple == n, turned, acc[4 + 2 * i])
                    acc[5 + 2 * i] = jnp.where(couple == (n - 1) % 64, turned, acc[5 + 2 * i])
            for n in range(10):
                gathered[n, at, :] = acc[n]
    r = base + 3 * levels
    send_rows(slice(r, r + 1), row_bottoms[0].astype(F32), row_bottoms[5].astype(F32))
    for q in range(r + 1, pay_a.shape[0]):
        zero_row = jnp.zeros((1, cols), F32)
        send_rows(slice(q, q + 1), zero_row, zero_row)

    lane = iota((rows, LANES), 1)
    couple = lane // 2
    even = lane % 2 == 0
    head = lane % (2 * tracers) == 0
    level_of = couple // tracers
    inside = couple < items

    def spread(xs):
        xs = [jnp.where(head, turn(x, by), 0.0) for x, by in xs]
        for by in (2, 4):
            turned = [turn(x, by) for x in xs]
            xs = [x + y for x, y in zip(xs, turned)]
        return xs

    def column_mask(c):
        col = bottom_v[:, c : c + 1] if c >= 0 else bottom_v[:, cols + c : cols + c + 1]
        ok = (level_of < jnp.broadcast_to(col, (rows, LANES))) & inside
        return jnp.where(ok, 1.0, 0.0)

    first_two, last_two, second, third_last, *coefs = [gathered[n] for n in range(10)]
    cells = [
        first_two, turn(first_two, -1), turn(second, -2),
        turn(third_last, 3), turn(last_two, 2), turn(last_two, 1),
    ]
    m = [column_mask(c) for c in (0, 1, 2, -3, -2, -1)]
    four = [(0, 0), (0, -1), (1, 2), (1, 1)]
    own_coefs = spread(
        [(coefs[i], by) for i, by in four]
        + [(coefs[2 + i], by) for i, by in four if by != -1]
        + [(coefs[4 + i], by) for i, by in four if by != -1]
    )
    jump_01 = (cells[1] - cells[0]) * (m[0] * m[1])
    jump_12 = (cells[2] - cells[1]) * (m[1] * m[2])
    jump_e0 = (cells[4] - cells[3]) * (m[3] * m[4])
    jump_e1 = (cells[5] - cells[4]) * (m[4] * m[5])
    zero = jnp.zeros((rows, LANES), F32)
    lows = (cells[5], own_coefs[3], own_coefs[9], cells[0], own_coefs[0], zero)
    highs = [turn(x, 1) for x in (jump_e1, own_coefs[6], m[5], jump_01, m[0])]
    highs.insert(4, zero)
    pays = [jnp.where(even, low, high) for low, high in zip(lows, highs)]
    for n in range(3):
        pay_c[n] = jnp.where(odd_lon, pays[3 + n], pays[n])
        pay_d[n] = jnp.where(odd_lon, pays[n], pays[3 + n])
    for n, x in enumerate([cells[0], cells[1], jump_12, cells[4], cells[5], jump_e0] + own_coefs):
        own_lon[n] = x


def pack(tracer, east_vel, north_vel, diff, east_slope, north_slope, bottom):
    tracers, levels, rows, cols = tracer.shape
    items = tracers * levels
    lat_rows = -(-(2 * items + 3 * levels + 1) // ROWS) * ROWS
    hbm = pl.BlockSpec(memory_space=pltpu.HBM)

    def body(*refs):
        pack_kernel(levels, tracers, rows, cols, "lon", "lat", *refs)

    shapes = [
        (lat_rows, cols),
        (lat_rows, cols),
        (3, rows, LANES),
        (3, rows, LANES),
        (16, rows, LANES),
        (6, items, cols),
        (10, levels, cols),
    ]
    return pl.pallas_call(
        body,
        name="pack_edges",
        in_specs=[hbm] * 7,
        out_specs=[pl.BlockSpec(memory_space=pltpu.VMEM)] * 12,
        out_shape=[pltpu.VMEM(x, F32) for x in shapes]
        + [pltpu.VMEM(x.shape, x.dtype) for x in (tracer, east_vel, diff, east_slope, bottom)],
        scratch_shapes=[
            pltpu.VMEM((4, levels, ROWS, cols), F32),
            pltpu.VMEM((10, rows, LANES), F32),
            pltpu.VMEM((ROWS // tracers * (tracers + 3), rows, LANES), F32),
            pltpu.SemaphoreType.DMA((levels * tracers // ROWS, 4)),
            pltpu.SemaphoreType.DMA((5,)),
        ],
        compiler_params=pltpu.CompilerParams(vmem_limit_bytes=VMEM_LIMIT),
        cost_estimate=pl.CostEstimate(flops=10**6, bytes_accessed=7 * 10**6, transcendentals=0),
    )(tracer, east_vel, north_vel, diff, east_slope, north_slope, bottom)


def interior_kernel(levels, tracers, rows, cols, span, *refs):
    tracer, east_vel, north_vel_hbm, diff, east_slope, north_slope_hbm, bottom, explicit = refs[:8]
    sources = (north_vel_hbm, north_slope_hbm)
    (
        north_vel,
        north_slope,
        sems,
        ring,
        ring_sum,
        step_here,
        step_west,
        bend_here,
        bend_east,
        flux_west,
        partial,
        north_part,
        open_at,
        coef,
    ) = refs[8:]
    first, stop = span()
    blocks = rows // ROWS
    halves = (slice(0, LANES), slice(LANES, 2 * LANES))
    lane = iota((ROWS, LANES), 1)
    sub = iota((ROWS, LANES), 0)

    def chunk(b):
        return slice(b * ROWS, (b + 1) * ROWS)

    def east_of(x):
        left, right = x
        turned = pltpu.roll(right, LANES - 1, axis=1)
        return (
            jnp.where(lane == LANES - 1, turned, pltpu.roll(left, LANES - 1, axis=1)),
            turned,
        )

    def west_of(x):
        left, right = x
        turned = pltpu.roll(left, 1, axis=1)
        return turned, jnp.where(lane == 0, turned, pltpu.roll(right, 1, axis=1))

    def up(x):
        return tuple(pltpu.roll(y, ROWS - 1, axis=0) for y in x)

    def down(x):
        return tuple(pltpu.roll(y, 1, axis=0) for y in x)

    def north_of(turned, turned_next):
        if turned_next is None:
            return turned
        return tuple(jnp.where(sub == ROWS - 1, n, y) for y, n in zip(turned, turned_next))

    def south_of(turned, turned_before):
        if turned_before is None:
            return turned
        return tuple(jnp.where(sub == 0, n, y) for y, n in zip(turned, turned_before))

    def load(ref, *index):
        *lead, b = index
        return tuple(ref[(*lead, chunk(b), h)] for h in halves)

    def save(ref, values, *index):
        *lead, b = index
        for h, x in zip(halves, values):
            ref[(*lead, chunk(b), h)] = x

    def sub2(x, y):
        return tuple(p - q for p, q in zip(x, y))

    def add2(x, y):
        return tuple(p + q for p, q in zip(x, y))

    def low2(x, y):
        return tuple(jnp.minimum(p, q) for p, q in zip(x, y))

    units = [(t, b) for b in range(blocks) for t in range(tracers)]

    def fetch(n, level):
        dst = (north_vel, north_slope)[n]
        return pltpu.make_async_copy(sources[n].at[level], dst.at[level], sems.at[n, level])

    def each_level(low, high, body):
        def run(level, carry):
            body(level)
            return carry

        lax.fori_loop(low, high, run, 0)

    def take_in(level, slot, out):
        at = jnp.clip(level, 0, levels - 1)
        depth = jnp.where(level < 0, levels, level)
        for b in range(blocks):
            sea = tuple(x > depth for x in load(bottom, b))
            for t in range(tracers):
                here = tuple(
                    jnp.where(s, x, 0.0) for s, x in zip(sea, load(tracer, t, at, b))
                )
                east = east_of(here)
                save(ring, here, slot, t, b)
                save(ring_sum, add2(here, east), slot, t, b)
                save(step_here, sub2(east, here), out, t, b)

    def take_steps(out):
        for t, b in units:
            save(step_west, west_of(load(step_here, out, t, b)), out, t, b)

    @pl.when(first < stop)
    def _():
        def begin(level):
            for n in range(2):
                fetch(n, level).start()

        each_level(first, stop, begin)
        depth = [load(bottom, b) for b in range(blocks)]
        ups, downs = [up(x) for x in depth], [down(x) for x in depth]
        east = [low2(x, east_of(x)) for x in depth]
        east_both = [low2(x, west_of(x)) for x in east]
        north = [
            low2(x, north_of(ups[b], ups[b + 1] if b + 1 < blocks else None))
            for b, x in enumerate(depth)
        ]
        north_downs = [down(x) for x in north]
        north_both = [
            low2(x, south_of(north_downs[b], north_downs[b - 1] if b else None))
            for b, x in enumerate(north)
        ]
        north_ups = [up(x) for x in north_both]
        for b in range(blocks):
            row = sub + b * ROWS
            inner_rows = (row > 0) & (row < rows - 2)
            inner = tuple(
                (lane + i * LANES > 0) & (lane + i * LANES < cols - 2) for i in range(2)
            )
            save(open_at, tuple(jnp.where(c, x, 0) for c, x in zip(inner, east[b])), 0, b)
            save(open_at, east_both[b], 1, b)
            save(open_at, east_of(east_both[b]), 2, b)
            save(open_at, tuple(jnp.where(inner_rows, x, 0) for x in north[b]), 3, b)
            save(open_at, north_both[b], 4, b)
            save(
                open_at,
                north_of(north_ups[b], north_ups[b + 1] if b + 1 < blocks else None),
                5,
                b,
            )
        take_in(first - 1, lax.rem(first + 2, 3), lax.rem(first + 1, 2))
        take_in(first, lax.rem(first, 3), lax.rem(first, 2))
        take_steps(lax.rem(first, 2))

    def one_level(level):
        now, later, before = lax.rem(level, 3), lax.rem(level + 1, 3), lax.rem(level + 2, 3)
        nth = lax.rem(level, 2)
        nth_next = 1 - nth
        for n in range(2):
            fetch(n, level).wait()

        for t, b in units:
            bend = tuple(
                minmod(x, y)
                for x, y in zip(load(step_here, nth, t, b), load(step_west, nth, t, b))
            )
            save(bend_here, bend, t, b)
            save(bend_east, east_of(bend), t, b)

        take_in(level + 1, later, nth_next)

        for b in range(blocks):
            here = load(diff, level, b)
            north = north_of(up(here), up(load(diff, level, min(b + 1, blocks - 1))))
            for way, other, vel, slope in (
                (0, east_of(here), east_vel, east_slope),
                (1, north, north_vel, north_slope),
            ):
                for i, h in enumerate(halves):
                    at = (chunk(b), h)
                    face = open_at[(3 * way, *at)] > level
                    speed = jnp.where(face, vel[(level, *at)], 0.0)
                    mean = jnp.where(face, 0.5 * (here[i] + other[i]), 0.0)
                    depth = jnp.where(
                        speed >= 0, open_at[(3 * way + 1, *at)], open_at[(3 * way + 2, *at)]
                    )
                    coef[(4 * way, *at)] = speed
                    coef[(4 * way + 1, *at)] = jnp.where(depth > level, limiter_weight(speed), 0.0)
                    coef[(4 * way + 2, *at)] = mean - jnp.minimum(speed, 0.0)
                    coef[(4 * way + 3, *at)] = 0.125 * slope[(level, *at)] * mean

        def face(way, b, here, step, bend, bend_other, tilt):
            out = []
            for i, h in enumerate(halves):
                at = (chunk(b), h)
                speed = coef[(4 * way, *at)]
                limited = jnp.where(speed >= 0, bend[i], bend_other[i])
                out.append(
                    (coef[(4 * way + 2, *at)] * step[i] - coef[(4 * way + 3, *at)] * tilt[i])
                    - (speed * here[i] + coef[(4 * way + 1, *at)] * limited)
                )
            return tuple(out)

        def north_faces(t):
            def stage(b):
                here = load(ring, now, t, b)
                tilt = sub2(load(ring, later, t, b), load(ring, before, t, b))
                return here, up(here), tilt, up(tilt)

            this = stage(0)
            step_before = flux_before = held = None
            for b in range(blocks + 1):
                if b < blocks:
                    nxt = stage(b + 1) if b + 1 < blocks else (None,) * 4
                    here, turned, tilt, tilt_turned = this
                    north = north_of(turned, nxt[1])
                    step = sub2(north, here)
                    step_turned = down(step)
                    bend = tuple(
                        minmod(x, y) for x, y in zip(step, south_of(step_turned, step_before))
                    )
                    bend_turned = up(bend)
                    step_before = step_turned
                if held is not None:
                    pb, p_here, p_step, p_bend, p_bend_turned, p_tilt = held
                    bend_n = north_of(p_bend_turned, bend_turned if b < blocks else None)
                    flux = face(1, pb, p_here, p_step, p_bend, bend_n, p_tilt)
                    flux_turned = down(flux)
                    if flux_before is None:
                        flux_s = tuple(jnp.where(sub == 0, 0.0, y) for y in flux_turned)
                    else:
                        flux_s = south_of(flux_turned, flux_before)
                    flux_before = flux_turned
                    save(north_part, add2(p_here, sub2(flux, flux_s)), t, pb)
                if b < blocks:
                    held = (
                        b, here, step, bend, bend_turned,
                        add2(tilt, north_of(tilt_turned, nxt[3])),
                    )
                    this = nxt

        for t in range(0, tracers, 2):
            north_faces(t)

        for t, b in units:
            flux = face(
                0,
                b,
                load(ring, now, t, b),
                load(step_here, nth, t, b),
                load(bend_here, t, b),
                load(bend_east, t, b),
                sub2(load(ring_sum, later, t, b), load(ring_sum, before, t, b)),
            )
            left, right = west_of(flux)
            save(flux_west, (jnp.where(lane == 0, 0.0, left), right), t, b)
            save(partial, flux, t, b)

        take_steps(nth_next)

        for t in range(1, tracers, 2):
            north_faces(t)

        for t, b in units:
            total = add2(
                load(north_part, t, b), sub2(load(partial, t, b), load(flux_west, t, b))
            )
            save(explicit, total, t, level, b)


    each_level(first, stop, one_level)


def interior(tracer, east_vel, north_vel, diff, east_slope, north_slope, bottom, span):
    tracers, levels, rows, cols = tracer.shape

    def body(*refs):
        interior_kernel(levels, tracers, rows, cols, span, *refs)

    plane = (tracers, rows, cols)
    field = pltpu.VMEM((levels, rows, cols), F32)
    args = (tracer, east_vel, north_vel, diff, east_slope, north_slope, bottom)
    hbm = pl.BlockSpec(memory_space=pltpu.HBM)
    vmem = pl.BlockSpec(memory_space=pltpu.VMEM)
    return pl.pallas_call(
        body,
        name="interior_faces",
        in_specs=[vmem, vmem, hbm, vmem, vmem, hbm, vmem],
        out_specs=vmem,
        out_shape=pltpu.VMEM(tracer.shape, F32),
        scratch_shapes=[
            field,
            field,
            pltpu.SemaphoreType.DMA((2, levels)),
            pltpu.VMEM((3, *plane), F32),
            pltpu.VMEM((3, *plane), F32),
            pltpu.VMEM((2, *plane), F32),
            pltpu.VMEM((2, *plane), F32),
            pltpu.VMEM(plane, F32),
            pltpu.VMEM(plane, F32),
            pltpu.VMEM(plane, F32),
            pltpu.VMEM(plane, F32),
            pltpu.VMEM(plane, F32),
            pltpu.VMEM((6, rows, cols), jnp.int32),
            pltpu.VMEM((8, rows, cols), F32),
        ],
        compiler_params=pltpu.CompilerParams(vmem_limit_bytes=VMEM_LIMIT),
        cost_estimate=pl.CostEstimate(
            flops=60 * tracer.size, bytes_accessed=12 * 10**6, transcendentals=0
        ),
    )(*args)


def edge_faces(m1, m2, m3, j0, j3, open1, open2, d1, d2, d3, v0, v1, s0, s1, tilt):
    j1 = (m2 - m1) * open1
    j2 = (m3 - m2) * open2
    t1, t2, t3 = tilt(m1), tilt(m2), tilt(m3)

    def face(low, high, behind, jump, ahead, opened, d_sum, vel, slope, tilts):
        speed = vel * opened
        forward = speed >= 0
        flux = speed * jnp.where(forward, low, high) + limiter_weight(speed) * minmod(
            jump, jnp.where(forward, behind, ahead)
        )
        return 0.5 * d_sum * (jump - 0.125 * slope * opened * tilts) - flux

    return (
        face(m1, m2, j0, j1, j2, open1, d1 + d2, v0, s0, t1 + t2),
        face(m2, m3, j1, j2, j3, open2, d2 + d3, v1, s1, t2 + t3),
    )


def solve_kernel(levels, tracers, rows, cols, lon_name, lat_name, lat_count, *refs):
    (
        explicit,
        vertical_hbm,
        bottom,
        got_a,
        got_b,
        got_c,
        got_d,
        own_lon,
        own_lat,
        own_lat_coef,
        out_hbm,
        field,
        vertical,
        fix_lon,
        fix_lat,
        south,
        north,
        pivots,
        in_sems,
        out_sems,
    ) = refs
    blocks = rows // ROWS
    items = levels * tracers
    base = 2 * items
    halves = (slice(0, LANES), slice(LANES, 2 * LANES))
    lane = iota((ROWS, LANES), 1)
    sub = iota((ROWS, LANES), 0)

    def rows_of(b):
        if isinstance(b, int):
            return pl.ds(b * ROWS, ROWS)
        return pl.ds(pl.multiple_of(b * ROWS, ROWS), ROWS)

    def fetch(b):
        at = rows_of(b)
        return pltpu.make_async_copy(
            vertical_hbm.at[:, at, :], vertical.at[:, at, :], in_sems.at[b]
        )

    def store(b):
        at = rows_of(b)
        return pltpu.make_async_copy(
            field.at[:, :, at, :], out_hbm.at[:, :, at, :], out_sems.at[b]
        )

    for b in range(blocks):
        fetch(b).start()

    def edges():
        odd_lon = lax.rem(lax.axis_index(lon_name), 2) == 1
        lat = lax.axis_index(lat_name)
        odd_lat = lax.rem(lat, 2) == 1
        top = lat == lat_count - 1
        even = lane % 2 == 0
        inside = lane < 2 * items
        level = lane // (2 * tracers)

        def tilt_lanes(x):
            return pltpu.roll(x, LANES - 2 * tracers, axis=1) - pltpu.roll(
                x, 2 * tracers, axis=1
            )

        for b in range(blocks):
            at = slice(b * ROWS, (b + 1) * ROWS)

            def mask(c):
                col = jnp.broadcast_to(bottom[at, c : c + 1], (ROWS, LANES))
                return jnp.where((level < col) & inside, 1.0, 0.0)

            def halves_of(pays):
                return pays, [pltpu.roll(x, LANES - 1, axis=1) for x in pays]

            c_got = [got_c[n, at, :] for n in range(3)]
            d_got = [got_d[n, at, :] for n in range(3)]
            from_west = [jnp.where(odd_lon, c, d) for c, d in zip(c_got, d_got)]
            from_east = [jnp.where(odd_lon, d, c) for c, d in zip(c_got, d_got)]
            own = [own_lon[n, at, :] for n in range(16)]
            (wm, wd, ws), (wj, wv, wk) = halves_of(from_west)
            m0, m1 = mask(0), mask(1)
            f0, f1 = edge_faces(
                wm, own[0], own[1], wj, own[2], wk * m0, m0 * m1,
                wd, own[6], own[7], wv, own[10], ws, own[13], tilt_lanes,
            )
            fix_lon[0, at, :] = jnp.where(
                even, (f1 - f0) * m0, pltpu.roll(-f1 * m1, 1, axis=1)
            )
            (em, ed, _), (ej, _, ek) = halves_of(from_east)
            m0, m1 = mask(cols - 2), mask(cols - 1)
            f0, f1 = edge_faces(
                own[3], own[4], em, own[5], ej, m0 * m1, m1 * ek,
                own[8], own[9], ed, own[11], own[12], own[14], own[15], tilt_lanes,
            )
            fix_lon[1, at, :] = jnp.where(
                even, f0 * m0, pltpu.roll((f1 - f0) * m1, 1, axis=1)
            )

        south[...] = jnp.where(odd_lat, got_a[...], got_b[...])

        @pl.when(jnp.logical_not(top))
        def _():
            north[...] = jnp.where(odd_lat, got_b[...], got_a[...])

        @pl.when(top)
        def _():
            mirror = LANES - 1 - lane
            for b in range(north.shape[0] // ROWS):
                at = slice(b * ROWS, (b + 1) * ROWS)
                for i in range(2):
                    north[at, halves[i]] = jnp.take_along_axis(
                        got_b[at, halves[1 - i]], mirror, axis=1, mode="promise_in_bounds"
                    )

        wide = iota((ROWS, cols), 0)
        sign = jnp.where(top, -1.0, 1.0)

        def spread_rows(ref, first, b):
            k = b * ROWS // tracers
            low, high = ref[first + k : first + k + 1, :], ref[first + k + 1 : first + k + 2, :]
            return jnp.where(
                wide < tracers,
                jnp.broadcast_to(low, (ROWS, cols)),
                jnp.broadcast_to(high, (ROWS, cols)),
            )

        def tilt_rows_of(read):
            def tilt(b):
                here = read(b)
                zeros = jnp.zeros_like(here)
                turned = pltpu.roll(here, tracers, axis=0)
                after = pltpu.roll(read(b + 1), tracers, axis=0) if b + 1 < items // ROWS else zeros
                before = pltpu.roll(read(b - 1), tracers, axis=0) if b else zeros
                return jnp.where(wide < tracers, turned, after) - jnp.where(
                    wide < tracers, before, turned
                )

            return tilt

        def own_row(n):
            return lambda b: own_lat[n, b * ROWS : (b + 1) * ROWS, :]

        def ghost_row(ref):
            return lambda b: ref[b * ROWS : (b + 1) * ROWS, :]

        for b in range(items // ROWS):
            at = slice(b * ROWS, (b + 1) * ROWS)
            past = slice(items + b * ROWS, items + (b + 1) * ROWS)
            level = (wide + b * ROWS) // tracers

            def mask(row):
                return jnp.where(level < jnp.broadcast_to(row, (ROWS, cols)), 1.0, 0.0)

            def coef(n):
                return spread_rows(own_lat_coef.at[n], 0, b)

            def ghost_mask(ref):
                row = ref[base + 3 * levels : base + 3 * levels + 1, :]
                return jnp.where(level.astype(F32) < jnp.broadcast_to(row, (ROWS, cols)), 1.0, 0.0)

            south_mask = jnp.where(lat > 0, ghost_mask(south), 0.0)

            def run(reads, j0, j3, open1, open2, d, v, s):
                tilts = [tilt_rows_of(r)(b) for r in reads]
                values = [r(b) for r in reads]
                lookup = dict(zip(map(id, values), tilts))
                return edge_faces(*values, j0, j3, open1, open2, *d, *v, *s,
                                  lambda x: lookup[id(x)])

            m0, m1 = mask(bottom[0:1, :]), mask(bottom[1:2, :])
            f0, f1 = run(
                (ghost_row(south), own_row(0), own_row(1)),
                jnp.where(lat > 0, south[past, :], 0.0), own_lat[2, at, :], south_mask * m0, m0 * m1,
                (spread_rows(south, base, b), coef(0), coef(1)),
                (spread_rows(south, base + levels, b), coef(4)),
                (spread_rows(south, base + 2 * levels, b), coef(7)),
            )
            fix_lat[0, at, :] = (f1 - f0) * m0
            fix_lat[1, at, :] = -f1 * m1
            m0 = mask(bottom[rows - 2 : rows - 1, :])
            m1 = mask(bottom[rows - 1 : rows, :])
            top_vel = coef(6)
            ghost_vel = spread_rows(north, base + levels, b)
            top_vel = jnp.where(top, 0.5 * (top_vel - ghost_vel), top_vel)
            f0, f1 = run(
                (own_row(3), own_row(4), ghost_row(north)),
                own_lat[5, at, :], sign * north[past, :], m0 * m1, m1 * ghost_mask(north),
                (coef(2), coef(3), spread_rows(north, base, b)),
                (coef(5), top_vel),
                (coef(8), coef(9)),
            )
            fix_lat[2, at, :] = f0 * m0
            fix_lat[3, at, :] = (f1 - f0) * m1

    edges()

    def one_block(step, side):
        at = rows_of(step)
        fetch(step).wait()

        def value_at(t, k, h):
            if not side:
                return explicit[t, k, at, h]
            n = k * tracers + t
            row0 = jnp.where(step == 0, 0, ROWS - 2)
            pick = jnp.where(step == 0, 0, 2)
            low = jnp.broadcast_to(fix_lat[pick, n : n + 1, h], (ROWS, LANES))
            high = jnp.broadcast_to(fix_lat[pick + 1, n : n + 1, h], (ROWS, LANES))
            return explicit[t, k, at, h] + jnp.where(
                sub == row0, low, jnp.where(sub == row0 + 1, high, 0.0)
            )

        depth = tuple(bottom[at, h] for h in halves)
        for i, h in enumerate(halves):
            ratio = above = None
            for k in range(levels):
                if k + 1 < levels:
                    below = jnp.where(depth[i] > k + 1, vertical[k, at, h], 0.0)
                if k == 0:
                    pivot = 1.0 + below
                elif k + 1 < levels:
                    pivot = (1.0 + above + below) + above * ratio
                else:
                    pivot = (1.0 + above) + above * ratio
                inverse = 1.0 / pivot
                pivots[0, k, :, h] = inverse
                if k:
                    pivots[1, k, :, h] = above
                if k + 1 < levels:
                    ratio = below * inverse
                    pivots[2, k, :, h] = ratio
                    above = below

        fixes = [fix_lon[i, at, :] for i in range(2)]
        for t in range(tracers):
            for i, h in enumerate(halves):
                begin = 0 if i == 0 else LANES - 2
                near = lane < 2 if i == 0 else lane >= LANES - 2
                values = []
                value = None
                for k in range(levels):
                    turn = (begin - 2 * (k * tracers + t)) % LANES
                    patch = pltpu.roll(fixes[i], turn, axis=1) if turn else fixes[i]
                    right = value_at(t, k, h) + jnp.where(near, patch, 0.0)
                    right = jnp.where(depth[i] > k, right, 0.0)
                    if k:
                        right = right + pivots[1, k, :, h] * value
                    value = right * pivots[0, k, :, h]
                    values.append(value)
                nxt = values[-1]
                field[t, levels - 1, at, h] = nxt
                for k in range(levels - 2, -1, -1):
                    nxt = values[k] + pivots[2, k, :, h] * nxt
                    field[t, k, at, h] = nxt
        store(step).start()

    @pl.loop(0, 2)
    def _(n):
        one_block(n * (blocks - 1), True)

    @pl.loop(1, blocks - 1)
    def _(step):
        one_block(step, False)

    for b in range(blocks):
        store(b).wait()


def solve(explicit, vertical, bottom, got, own):
    tracers, levels, rows, cols = explicit.shape
    items = levels * tracers
    lat_rows = got[0].shape[0]
    lat_count = lax.axis_size("lat")
    blocks = rows // ROWS

    def body(*refs):
        solve_kernel(levels, tracers, rows, cols, "lon", "lat", lat_count, *refs)

    hbm = pl.BlockSpec(memory_space=pltpu.HBM)
    vmem = pl.BlockSpec(memory_space=pltpu.VMEM)
    return pl.pallas_call(
        body,
        name="edges_and_solve",
        in_specs=[vmem, hbm] + [vmem] * 8,
        out_specs=hbm,
        out_shape=jax.ShapeDtypeStruct(explicit.shape, F32),
        scratch_shapes=[
            pltpu.VMEM(explicit.shape, F32),
            pltpu.VMEM(vertical.shape, F32),
            pltpu.VMEM((2, rows, LANES), F32),
            pltpu.VMEM((4, items, cols), F32),
            pltpu.VMEM((lat_rows, cols), F32),
            pltpu.VMEM((lat_rows, cols), F32),
            pltpu.VMEM((3, levels, ROWS, cols), F32),
            pltpu.SemaphoreType.DMA((blocks,)),
            pltpu.SemaphoreType.DMA((blocks,)),
        ],
        compiler_params=pltpu.CompilerParams(vmem_limit_bytes=SOLVE_LIMIT),
        cost_estimate=pl.CostEstimate(
            flops=20 * explicit.size, bytes_accessed=8 * 10**6, transcendentals=0
        ),
    )(explicit, vertical, bottom, *got, *own)


def local(
    tracer,
    east_velocity,
    north_velocity,
    diffusivity,
    east_slope,
    north_slope,
    vertical_diffusivity,
    sea_mask,
    bottom,
):
    lon, lat = lax.axis_size("lon"), lax.axis_size("lat")
    levels = tracer.shape[1]
    args = tuple(
        pltpu.with_memory_space_constraint(x, pltpu.HBM)
        for x in (
            tracer, east_velocity, north_velocity, diffusivity, east_slope, north_slope, bottom
        )
    )
    north = (args[2], args[5])
    pay_a, pay_b, pay_c, pay_d, *own, held, held_vel, held_diff, held_slope, depth = pack(
        *args
    )

    def swap(pairs):
        return [p for a, b in pairs for p in ((a, b), (b, a))]

    def at(i, j):
        return i * lat + j

    near_lat = swap([(j, j + 1) for j in range(0, lat, 2)])
    far_lat = swap([(at(i, j), at(i, j + 1)) for i in range(lon) for j in range(1, lat - 1, 2)])
    far_lat += [(at(i, lat - 1), at(lon - 1 - i, lat - 1)) for i in range(lon)]
    far_lat += swap([(at(i, 0), at(i + 1, 0)) for i in range(0, lon, 2)])
    near_lon = swap([(i, i + 1) for i in range(0, lon, 2)])
    far_lon = swap([(i, (i + 1) % lon) for i in range(1, lon, 2)])
    got_a = lax.ppermute(pay_a, "lat", near_lat)
    got_c = lax.ppermute(pay_c, "lon", near_lon)
    got_b = lax.ppermute(pay_b, ("lon", "lat"), far_lat)
    got_d = lax.ppermute(pay_d, "lon", far_lon)
    explicit = interior(
        held, held_vel, north[0], held_diff, held_slope, north[1], depth,
        lambda: (0, levels),
    )
    return solve(
        explicit, vertical_diffusivity, depth, (got_a, got_b, got_c, got_d), tuple(own)
    )


def solution(mesh):
    field = P(None, "lat", "lon")
    placed = (
        P(None, None, "lat", "lon"),
        field,
        field,
        field,
        field,
        field,
        field,
        field,
        P("lat", "lon"),
    )
    return jax.shard_map(
        local, mesh=mesh, in_specs=placed, out_specs=P(None, None, "lat", "lon"), check_vma=False
    )
```

```python
import jax
import jax.numpy as jnp
from jax import lax
from jax.experimental import pallas as pl
from jax.experimental.pallas import tpu as pltpu
from jax.sharding import PartitionSpec as P

F32 = jnp.float32
LANES = 128
ROWS = 8
VMEM_LIMIT = 36 << 20
SOLVE_LIMIT = 32 << 20


def iota(shape, dim):
    return lax.broadcasted_iota(jnp.int32, shape, dim)


def minmod(first, second):
    return jnp.minimum(
        jnp.maximum(second, jnp.minimum(first, 0.0)), jnp.maximum(first, 0.0)
    )


def limiter_weight(speed):
    size = jnp.abs(speed)
    return 0.5 * size * (1.0 - size)


def pack_kernel(levels, tracers, rows, cols, lon_name, lat_name, *refs):
    sources = refs[:7]
    (
        pay_a,
        pay_b,
        pay_c,
        pay_d,
        own_lon,
        own_lat,
        own_lat_coef,
        tracer_v,
        east_vel_v,
        diff_v,
        east_slope_v,
        bottom_v,
        north_vel_v,
        north_slope_v,
        open_at,
        explicit,
        ring,
        ring_sum,
        step_here,
        step_west,
        north_v,
        gathered,
        turned_v,
        sems,
        row_sems,
        north_sems,
    ) = refs[7:33]
    scratch = refs[33:]
    tracer_hbm, east_vel_hbm, north_vel_hbm, diff_hbm, east_slope_hbm, north_slope_hbm = sources[:6]
    items = levels * tracers
    group = ROWS // tracers
    groups = levels // group
    last = rows - ROWS
    right = cols - LANES
    base = 2 * items
    row_copies = [pltpu.make_async_copy(sources[6], bottom_v, row_sems.at[0])]
    for n, (src, start) in enumerate(
        ((north_vel_hbm, 0), (north_vel_hbm, last), (north_slope_hbm, 0), (north_slope_hbm, last))
    ):
        row_copies.append(
            pltpu.make_async_copy(
                src.at[:, pl.ds(start, ROWS), :], north_v.at[n], row_sems.at[n + 1]
            )
        )
    copies = []
    for g in range(groups):
        span = pl.ds(g * group, group)
        fetch = [
            pltpu.make_async_copy(
                tracer_hbm.at[:, span], tracer_v.at[:, span], sems.at[g, 0]
            )
        ]
        for n, (src, dst) in enumerate(
            ((diff_hbm, diff_v), (east_vel_hbm, east_vel_v), (east_slope_hbm, east_slope_v))
        ):
            fetch.append(pltpu.make_async_copy(src.at[span], dst.at[span], sems.at[g, n + 1]))
        copies.append(fetch)
    row_copies[0].start()
    for copy in copies[0]:
        copy.start()
    for copy in row_copies[1:]:
        copy.start()
    for fetch in copies[1:]:
        for copy in fetch:
            copy.start()

    lane = iota((ROWS, LANES), 1)
    couple = lane // 2
    even = lane % 2 == 0
    left_side = lane < 64
    sub = iota((ROWS, cols), 0)
    row_at = (0, 1, 2, rows - 3, rows - 2, rows - 1)
    odd_lon = lax.rem(lax.axis_index(lon_name), 2) == 1
    odd_lat = lax.rem(lax.axis_index(lat_name), 2) == 1
    chunks = [slice(r * ROWS, (r + 1) * ROWS) for r in range(rows // ROWS)]

    def turn(x, by):
        by = by % LANES
        return pltpu.roll(x, by, axis=1) if by else x

    def send_rows(at, low, top):
        pay_a[at, :] = jnp.where(odd_lat, low, top)
        pay_b[at, :] = jnp.where(odd_lat, top, low)

    row_copies[0].wait()
    row_bottoms = [bottom_v[r : r + 1, :] for r in row_at]
    north_copies = [
        pltpu.make_async_copy(north_vel_hbm, north_vel_v, north_sems.at[0]),
        pltpu.make_async_copy(north_slope_hbm, north_slope_v, north_sems.at[1]),
    ]
    for g in range(groups):
        for copy in copies[g]:
            copy.wait()
        if g == groups - 1:
            for copy in north_copies:
                copy.start()
        for k in range(g * group, (g + 1) * group):
            j = (k - g * group) * (tracers + 3)
            for at in chunks:
                sea = jnp.where(left_side, bottom_v[at, :LANES], bottom_v[at, right:]) > k
                for t in range(tracers):
                    both = jnp.where(
                        left_side, tracer_v[t, k, at, :LANES], tracer_v[t, k, at, right:]
                    )
                    turned_v[j + t, at, :] = turn(
                        jnp.where(sea, both, 0.0), 2 * (k * tracers + t)
                    )
                for i, ref in enumerate((diff_v, east_vel_v, east_slope_v)):
                    both = jnp.where(left_side, ref[k, at, :LANES], ref[k, at, right:])
                    turned_v[j + tracers + i, at, :] = turn(both, 2 * k * tracers)
        first = g * group
        x = []
        m = []
        level = sub // tracers + first
        for c, r in enumerate(row_at):
            rows_in = jnp.broadcast_to(tracer_v[0, first, r : r + 1, :], (ROWS, cols))
            for q in range(1, ROWS):
                row = tracer_v[q % tracers, first + q // tracers, r : r + 1, :]
                rows_in = jnp.where(sub == q, jnp.broadcast_to(row, (ROWS, cols)), rows_in)
            m.append(
                jnp.where(level < jnp.broadcast_to(row_bottoms[c], (ROWS, cols)), 1.0, 0.0)
            )
            x.append(rows_in * m[c])
        at = pl.ds(g * ROWS, ROWS)
        for n, y in enumerate(
            (
                x[0],
                x[1],
                (x[2] - x[1]) * (m[1] * m[2]),
                x[4],
                x[5],
                (x[4] - x[3]) * (m[3] * m[4]),
            )
        ):
            own_lat[n, at, :] = y
        send_rows(at, x[0], x[5])
        send_rows(
            pl.ds(items + g * ROWS, ROWS),
            (x[1] - x[0]) * (m[0] * m[1]),
            (x[5] - x[4]) * (m[4] * m[5]),
        )
        if g == 0:
            for copy in row_copies[1:]:
                copy.wait()
        for k in range(first, first + group):
            values = (
                diff_v[k, 0:1, :],
                diff_v[k, 1:2, :],
                diff_v[k, rows - 2 : rows - 1, :],
                diff_v[k, rows - 1 : rows, :],
                north_v[0, k, 0:1, :],
                north_v[1, k, 6:7, :],
                north_v[1, k, 7:8, :],
                north_v[2, k, 0:1, :],
                north_v[3, k, 6:7, :],
                north_v[3, k, 7:8, :],
            )
            for n, y in enumerate(values):
                own_lat_coef[n, k : k + 1, :] = y
            for n, top in enumerate((values[3], values[6], values[9])):
                low = values[0] if n == 0 else jnp.zeros_like(top)
                r = base + n * levels + k
                send_rows(slice(r, r + 1), low, top)
        for at in chunks:
            acc = [gathered[n, at, :] if g else jnp.zeros((ROWS, LANES), F32) for n in range(10)]
            for k in range(first, first + group):
                j = (k - first) * (tracers + 3)
                for t in range(tracers):
                    n = k * tracers + t
                    turned = turned_v[j + t, at, :]
                    acc[0] = jnp.where(couple == n, turned, acc[0])
                    acc[1] = jnp.where(couple == (n - 1) % 64, turned, acc[1])
                    acc[2] = jnp.where(lane == 2 * n + 2, turned, acc[2])
                    acc[3] = jnp.where(lane == (2 * n - 3) % LANES, turned, acc[3])
                n = k * tracers
                for i in range(3):
                    turned = turned_v[j + tracers + i, at, :]
                    acc[4 + 2 * i] = jnp.where(couple == n, turned, acc[4 + 2 * i])
                    acc[5 + 2 * i] = jnp.where(couple == (n - 1) % 64, turned, acc[5 + 2 * i])
            for n in range(10):
                gathered[n, at, :] = acc[n]
    r = base + 3 * levels
    send_rows(slice(r, r + 1), row_bottoms[0].astype(F32), row_bottoms[5].astype(F32))
    for q in range(r + 1, pay_a.shape[0]):
        zero_row = jnp.zeros((1, cols), F32)
        send_rows(slice(q, q + 1), zero_row, zero_row)

    lane = iota((rows, LANES), 1)
    couple = lane // 2
    even = lane % 2 == 0
    head = lane % (2 * tracers) == 0
    level_of = couple // tracers
    inside = couple < items

    def spread(xs):
        xs = [jnp.where(head, turn(x, by), 0.0) for x, by in xs]
        for by in (2, 4):
            turned = [turn(x, by) for x in xs]
            xs = [x + y for x, y in zip(xs, turned)]
        return xs

    def column_mask(c):
        col = bottom_v[:, c : c + 1] if c >= 0 else bottom_v[:, cols + c : cols + c + 1]
        ok = (level_of < jnp.broadcast_to(col, (rows, LANES))) & inside
        return jnp.where(ok, 1.0, 0.0)

    first_two, last_two, second, third_last, *coefs = [gathered[n] for n in range(10)]
    cells = [
        first_two, turn(first_two, -1), turn(second, -2),
        turn(third_last, 3), turn(last_two, 2), turn(last_two, 1),
    ]
    m = [column_mask(c) for c in (0, 1, 2, -3, -2, -1)]
    four = [(0, 0), (0, -1), (1, 2), (1, 1)]
    own_coefs = spread(
        [(coefs[i], by) for i, by in four]
        + [(coefs[2 + i], by) for i, by in four if by != -1]
        + [(coefs[4 + i], by) for i, by in four if by != -1]
    )
    jump_01 = (cells[1] - cells[0]) * (m[0] * m[1])
    jump_12 = (cells[2] - cells[1]) * (m[1] * m[2])
    jump_e0 = (cells[4] - cells[3]) * (m[3] * m[4])
    jump_e1 = (cells[5] - cells[4]) * (m[4] * m[5])
    zero = jnp.zeros((rows, LANES), F32)
    lows = (cells[5], own_coefs[3], own_coefs[9], cells[0], own_coefs[0], zero)
    highs = [turn(x, 1) for x in (jump_e1, own_coefs[6], m[5], jump_01, m[0])]
    highs.insert(4, zero)
    pays = [jnp.where(even, low, high) for low, high in zip(lows, highs)]
    for n in range(3):
        pay_c[n] = jnp.where(odd_lon, pays[3 + n], pays[n])
        pay_d[n] = jnp.where(odd_lon, pays[n], pays[3 + n])
    for n, x in enumerate([cells[0], cells[1], jump_12, cells[4], cells[5], jump_e0] + own_coefs):
        own_lon[n] = x

    for copy in north_copies:
        copy.wait()
    interior_stage(
        levels, tracers, rows, 0, levels_ahead(levels), True,
        (
            tracer_v, east_vel_v, north_vel_v, diff_v, east_slope_v, north_slope_v, bottom_v,
            open_at, explicit, ring, ring_sum, step_here, step_west, *scratch,
        ),
    )


def pack(tracer, east_vel, north_vel, diff, east_slope, north_slope, bottom):
    tracers, levels, rows, cols = tracer.shape
    items = tracers * levels
    lat_rows = -(-(2 * items + 3 * levels + 1) // ROWS) * ROWS
    hbm = pl.BlockSpec(memory_space=pltpu.HBM)

    def body(*refs):
        pack_kernel(levels, tracers, rows, cols, "lon", "lat", *refs)

    shapes = [
        (lat_rows, cols),
        (lat_rows, cols),
        (3, rows, LANES),
        (3, rows, LANES),
        (16, rows, LANES),
        (6, items, cols),
        (10, levels, cols),
    ]
    return pl.pallas_call(
        body,
        name="pack_edges",
        in_specs=[hbm] * 7,
        out_specs=[pl.BlockSpec(memory_space=pltpu.VMEM)] * 20,
        out_shape=[pltpu.VMEM(x, F32) for x in shapes]
        + [
            pltpu.VMEM(x.shape, x.dtype)
            for x in (tracer, east_vel, diff, east_slope, bottom, north_vel, north_slope)
        ]
        + [pltpu.VMEM((6, rows, cols), jnp.int32), pltpu.VMEM(tracer.shape, F32)]
        + [pltpu.VMEM((n, tracers, rows, cols), F32) for n in (3, 3, 2, 2)],
        scratch_shapes=[
            pltpu.VMEM((4, levels, ROWS, cols), F32),
            pltpu.VMEM((10, rows, LANES), F32),
            pltpu.VMEM((ROWS // tracers * (tracers + 3), rows, LANES), F32),
            pltpu.SemaphoreType.DMA((levels * tracers // ROWS, 4)),
            pltpu.SemaphoreType.DMA((5,)),
            pltpu.SemaphoreType.DMA((2,)),
            *stage_scratch(tracers, rows, cols),
        ],
        compiler_params=pltpu.CompilerParams(vmem_limit_bytes=VMEM_LIMIT),
        cost_estimate=pl.CostEstimate(flops=10**6, bytes_accessed=7 * 10**6, transcendentals=0),
    )(tracer, east_vel, north_vel, diff, east_slope, north_slope, bottom)


def interior_stage(levels, tracers, rows, first, stop, fresh, refs):
    (
        tracer,
        east_vel,
        north_vel,
        diff,
        east_slope,
        north_slope,
        bottom,
        open_at,
        explicit,
        ring,
        ring_sum,
        step_here,
        step_west,
        bend_here,
        bend_east,
        flux_west,
        partial,
        north_part,
        coef,
    ) = refs
    cols = 2 * LANES
    blocks = rows // ROWS
    halves = (slice(0, LANES), slice(LANES, 2 * LANES))
    lane = iota((ROWS, LANES), 1)
    sub = iota((ROWS, LANES), 0)

    def chunk(b):
        return slice(b * ROWS, (b + 1) * ROWS)

    def east_of(x):
        left, right = x
        turned = pltpu.roll(right, LANES - 1, axis=1)
        return (
            jnp.where(lane == LANES - 1, turned, pltpu.roll(left, LANES - 1, axis=1)),
            turned,
        )

    def west_of(x):
        left, right = x
        turned = pltpu.roll(left, 1, axis=1)
        return turned, jnp.where(lane == 0, turned, pltpu.roll(right, 1, axis=1))

    def up(x):
        return tuple(pltpu.roll(y, ROWS - 1, axis=0) for y in x)

    def down(x):
        return tuple(pltpu.roll(y, 1, axis=0) for y in x)

    def north_of(turned, turned_next):
        if turned_next is None:
            return turned
        return tuple(jnp.where(sub == ROWS - 1, n, y) for y, n in zip(turned, turned_next))

    def south_of(turned, turned_before):
        if turned_before is None:
            return turned
        return tuple(jnp.where(sub == 0, n, y) for y, n in zip(turned, turned_before))

    def load(ref, *index):
        *lead, b = index
        return tuple(ref[(*lead, chunk(b), h)] for h in halves)

    def save(ref, values, *index):
        *lead, b = index
        for h, x in zip(halves, values):
            ref[(*lead, chunk(b), h)] = x

    def sub2(x, y):
        return tuple(p - q for p, q in zip(x, y))

    def add2(x, y):
        return tuple(p + q for p, q in zip(x, y))

    def low2(x, y):
        return tuple(jnp.minimum(p, q) for p, q in zip(x, y))

    units = [(t, b) for b in range(blocks) for t in range(tracers)]

    def each_level(low, high, body):
        def run(level, carry):
            body(level)
            return carry

        lax.fori_loop(low, high, run, 0)

    def take_in(level, slot, out):
        at = jnp.clip(level, 0, levels - 1)
        depth = jnp.where(level < 0, levels, level)
        for b in range(blocks):
            sea = tuple(x > depth for x in load(bottom, b))
            for t in range(tracers):
                here = tuple(
                    jnp.where(s, x, 0.0) for s, x in zip(sea, load(tracer, t, at, b))
                )
                east = east_of(here)
                save(ring, here, slot, t, b)
                save(ring_sum, add2(here, east), slot, t, b)
                save(step_here, sub2(east, here), out, t, b)

    def take_steps(out):
        for t, b in units:
            save(step_west, west_of(load(step_here, out, t, b)), out, t, b)

    if fresh:
        depth = [load(bottom, b) for b in range(blocks)]
        ups, downs = [up(x) for x in depth], [down(x) for x in depth]
        east = [low2(x, east_of(x)) for x in depth]
        east_both = [low2(x, west_of(x)) for x in east]
        north = [
            low2(x, north_of(ups[b], ups[b + 1] if b + 1 < blocks else None))
            for b, x in enumerate(depth)
        ]
        north_downs = [down(x) for x in north]
        north_both = [
            low2(x, south_of(north_downs[b], north_downs[b - 1] if b else None))
            for b, x in enumerate(north)
        ]
        north_ups = [up(x) for x in north_both]
        for b in range(blocks):
            row = sub + b * ROWS
            inner_rows = (row > 0) & (row < rows - 2)
            inner = tuple(
                (lane + i * LANES > 0) & (lane + i * LANES < cols - 2) for i in range(2)
            )
            save(open_at, tuple(jnp.where(c, x, 0) for c, x in zip(inner, east[b])), 0, b)
            save(open_at, east_both[b], 1, b)
            save(open_at, east_of(east_both[b]), 2, b)
            save(open_at, tuple(jnp.where(inner_rows, x, 0) for x in north[b]), 3, b)
            save(open_at, north_both[b], 4, b)
            save(
                open_at,
                north_of(north_ups[b], north_ups[b + 1] if b + 1 < blocks else None),
                5,
                b,
            )
        take_in(-1, 2, 1)
        take_in(0, 0, 0)
        take_steps(0)

    def one_level(level):
        now, later, before = lax.rem(level, 3), lax.rem(level + 1, 3), lax.rem(level + 2, 3)
        nth = lax.rem(level, 2)
        nth_next = 1 - nth
        for t, b in units:
            bend = tuple(
                minmod(x, y)
                for x, y in zip(load(step_here, nth, t, b), load(step_west, nth, t, b))
            )
            save(bend_here, bend, t, b)
            save(bend_east, east_of(bend), t, b)

        take_in(level + 1, later, nth_next)

        for b in range(blocks):
            here = load(diff, level, b)
            north = north_of(up(here), up(load(diff, level, min(b + 1, blocks - 1))))
            for way, other, vel, slope in (
                (0, east_of(here), east_vel, east_slope),
                (1, north, north_vel, north_slope),
            ):
                for i, h in enumerate(halves):
                    at = (chunk(b), h)
                    face = open_at[(3 * way, *at)] > level
                    speed = jnp.where(face, vel[(level, *at)], 0.0)
                    mean = jnp.where(face, 0.5 * (here[i] + other[i]), 0.0)
                    depth = jnp.where(
                        speed >= 0, open_at[(3 * way + 1, *at)], open_at[(3 * way + 2, *at)]
                    )
                    coef[(4 * way, *at)] = speed
                    coef[(4 * way + 1, *at)] = jnp.where(depth > level, limiter_weight(speed), 0.0)
                    coef[(4 * way + 2, *at)] = mean - jnp.minimum(speed, 0.0)
                    coef[(4 * way + 3, *at)] = 0.125 * slope[(level, *at)] * mean

        def face(way, b, here, step, bend, bend_other, tilt):
            out = []
            for i, h in enumerate(halves):
                at = (chunk(b), h)
                speed = coef[(4 * way, *at)]
                limited = jnp.where(speed >= 0, bend[i], bend_other[i])
                out.append(
                    (coef[(4 * way + 2, *at)] * step[i] - coef[(4 * way + 3, *at)] * tilt[i])
                    - (speed * here[i] + coef[(4 * way + 1, *at)] * limited)
                )
            return tuple(out)

        def north_faces(t):
            def stage(b):
                here = load(ring, now, t, b)
                tilt = sub2(load(ring, later, t, b), load(ring, before, t, b))
                return here, up(here), tilt, up(tilt)

            this = stage(0)
            step_before = flux_before = held = None
            for b in range(blocks + 1):
                if b < blocks:
                    nxt = stage(b + 1) if b + 1 < blocks else (None,) * 4
                    here, turned, tilt, tilt_turned = this
                    north = north_of(turned, nxt[1])
                    step = sub2(north, here)
                    step_turned = down(step)
                    bend = tuple(
                        minmod(x, y) for x, y in zip(step, south_of(step_turned, step_before))
                    )
                    bend_turned = up(bend)
                    step_before = step_turned
                if held is not None:
                    pb, p_here, p_step, p_bend, p_bend_turned, p_tilt = held
                    bend_n = north_of(p_bend_turned, bend_turned if b < blocks else None)
                    flux = face(1, pb, p_here, p_step, p_bend, bend_n, p_tilt)
                    flux_turned = down(flux)
                    if flux_before is None:
                        flux_s = tuple(jnp.where(sub == 0, 0.0, y) for y in flux_turned)
                    else:
                        flux_s = south_of(flux_turned, flux_before)
                    flux_before = flux_turned
                    save(north_part, add2(p_here, sub2(flux, flux_s)), t, pb)
                if b < blocks:
                    held = (
                        b, here, step, bend, bend_turned,
                        add2(tilt, north_of(tilt_turned, nxt[3])),
                    )
                    this = nxt

        for t in range(0, tracers, 2):
            north_faces(t)

        for t, b in units:
            flux = face(
                0,
                b,
                load(ring, now, t, b),
                load(step_here, nth, t, b),
                load(bend_here, t, b),
                load(bend_east, t, b),
                sub2(load(ring_sum, later, t, b), load(ring_sum, before, t, b)),
            )
            left, right = west_of(flux)
            save(flux_west, (jnp.where(lane == 0, 0.0, left), right), t, b)
            save(partial, flux, t, b)

        take_steps(nth_next)

        for t in range(1, tracers, 2):
            north_faces(t)

        for t, b in units:
            total = add2(
                load(north_part, t, b), sub2(load(partial, t, b), load(flux_west, t, b))
            )
            save(explicit, total, t, level, b)


    each_level(first, stop, one_level)


def stage_scratch(tracers, rows, cols):
    return [pltpu.VMEM((tracers, rows, cols), F32)] * 5 + [pltpu.VMEM((8, rows, cols), F32)]


def levels_ahead(levels):
    lead = lax.axis_size("lon") // 4
    early = jnp.maximum(lead - lax.axis_index("lon") // 2, 0)
    return (levels * early) // (2 * lead)


def interior_rest(held, state):
    tracers, levels, rows, cols = held[0].shape

    def body(*refs):
        given, changed, scratch = refs[:8], refs[13:18], refs[18:]
        interior_stage(
            levels, tracers, rows, levels_ahead(levels), levels, False,
            (*given, *changed, *scratch),
        )

    vmem = pl.BlockSpec(memory_space=pltpu.VMEM)
    return pl.pallas_call(
        body,
        name="interior_faces",
        in_specs=[vmem] * 13,
        out_specs=[vmem] * 5,
        out_shape=[pltpu.VMEM(x.shape, F32) for x in state],
        input_output_aliases={8 + n: n for n in range(5)},
        scratch_shapes=stage_scratch(tracers, rows, cols),
        compiler_params=pltpu.CompilerParams(vmem_limit_bytes=VMEM_LIMIT),
        cost_estimate=pl.CostEstimate(
            flops=60 * held[0].size, bytes_accessed=12 * 10**6, transcendentals=0
        ),
    )(*held, *state)[0]


def edge_faces(m1, m2, m3, j0, j3, open1, open2, d1, d2, d3, v0, v1, s0, s1, tilt):
    j1 = (m2 - m1) * open1
    j2 = (m3 - m2) * open2
    t1, t2, t3 = tilt(m1), tilt(m2), tilt(m3)

    def face(low, high, behind, jump, ahead, opened, d_sum, vel, slope, tilts):
        speed = vel * opened
        forward = speed >= 0
        flux = speed * jnp.where(forward, low, high) + limiter_weight(speed) * minmod(
            jump, jnp.where(forward, behind, ahead)
        )
        return 0.5 * d_sum * (jump - 0.125 * slope * opened * tilts) - flux

    return (
        face(m1, m2, j0, j1, j2, open1, d1 + d2, v0, s0, t1 + t2),
        face(m2, m3, j1, j2, j3, open2, d2 + d3, v1, s1, t2 + t3),
    )


def solve_kernel(levels, tracers, rows, cols, lon_name, lat_name, lat_count, *refs):
    (
        explicit,
        vertical_hbm,
        bottom,
        got_a,
        got_b,
        got_c,
        got_d,
        own_lon,
        own_lat,
        own_lat_coef,
        out_hbm,
        field,
        vertical,
        fix_lon,
        fix_lat,
        south,
        north,
        pivots,
        in_sems,
        out_sems,
    ) = refs
    blocks = rows // ROWS
    items = levels * tracers
    base = 2 * items
    halves = (slice(0, LANES), slice(LANES, 2 * LANES))
    lane = iota((ROWS, LANES), 1)
    sub = iota((ROWS, LANES), 0)

    def rows_of(b):
        if isinstance(b, int):
            return pl.ds(b * ROWS, ROWS)
        return pl.ds(pl.multiple_of(b * ROWS, ROWS), ROWS)

    def fetch(b):
        at = rows_of(b)
        return pltpu.make_async_copy(
            vertical_hbm.at[:, at, :], vertical.at[:, at, :], in_sems.at[b]
        )

    def store(b):
        at = rows_of(b)
        return pltpu.make_async_copy(
            field.at[:, :, at, :], out_hbm.at[:, :, at, :], out_sems.at[b]
        )

    for b in range(blocks):
        fetch(b).start()

    def edges():
        odd_lon = lax.rem(lax.axis_index(lon_name), 2) == 1
        lat = lax.axis_index(lat_name)
        odd_lat = lax.rem(lat, 2) == 1
        top = lat == lat_count - 1
        even = lane % 2 == 0
        inside = lane < 2 * items
        level = lane // (2 * tracers)

        def tilt_lanes(x):
            return pltpu.roll(x, LANES - 2 * tracers, axis=1) - pltpu.roll(
                x, 2 * tracers, axis=1
            )

        for b in range(blocks):
            at = slice(b * ROWS, (b + 1) * ROWS)

            def mask(c):
                col = jnp.broadcast_to(bottom[at, c : c + 1], (ROWS, LANES))
                return jnp.where((level < col) & inside, 1.0, 0.0)

            def halves_of(pays):
                return pays, [pltpu.roll(x, LANES - 1, axis=1) for x in pays]

            c_got = [got_c[n, at, :] for n in range(3)]
            d_got = [got_d[n, at, :] for n in range(3)]
            from_west = [jnp.where(odd_lon, c, d) for c, d in zip(c_got, d_got)]
            from_east = [jnp.where(odd_lon, d, c) for c, d in zip(c_got, d_got)]
            own = [own_lon[n, at, :] for n in range(16)]
            (wm, wd, ws), (wj, wv, wk) = halves_of(from_west)
            m0, m1 = mask(0), mask(1)
            f0, f1 = edge_faces(
                wm, own[0], own[1], wj, own[2], wk * m0, m0 * m1,
                wd, own[6], own[7], wv, own[10], ws, own[13], tilt_lanes,
            )
            fix_lon[0, at, :] = jnp.where(
                even, (f1 - f0) * m0, pltpu.roll(-f1 * m1, 1, axis=1)
            )
            (em, ed, _), (ej, _, ek) = halves_of(from_east)
            m0, m1 = mask(cols - 2), mask(cols - 1)
            f0, f1 = edge_faces(
                own[3], own[4], em, own[5], ej, m0 * m1, m1 * ek,
                own[8], own[9], ed, own[11], own[12], own[14], own[15], tilt_lanes,
            )
            fix_lon[1, at, :] = jnp.where(
                even, f0 * m0, pltpu.roll((f1 - f0) * m1, 1, axis=1)
            )

        south[...] = jnp.where(odd_lat, got_a[...], got_b[...])

        @pl.when(jnp.logical_not(top))
        def _():
            north[...] = jnp.where(odd_lat, got_b[...], got_a[...])

        @pl.when(top)
        def _():
            mirror = LANES - 1 - lane
            for b in range(north.shape[0] // ROWS):
                at = slice(b * ROWS, (b + 1) * ROWS)
                for i in range(2):
                    north[at, halves[i]] = jnp.take_along_axis(
                        got_b[at, halves[1 - i]], mirror, axis=1, mode="promise_in_bounds"
                    )

        wide = iota((ROWS, cols), 0)
        sign = jnp.where(top, -1.0, 1.0)

        def spread_rows(ref, first, b):
            k = b * ROWS // tracers
            low, high = ref[first + k : first + k + 1, :], ref[first + k + 1 : first + k + 2, :]
            return jnp.where(
                wide < tracers,
                jnp.broadcast_to(low, (ROWS, cols)),
                jnp.broadcast_to(high, (ROWS, cols)),
            )

        def tilt_rows_of(read):
            def tilt(b):
                here = read(b)
                zeros = jnp.zeros_like(here)
                turned = pltpu.roll(here, tracers, axis=0)
                after = pltpu.roll(read(b + 1), tracers, axis=0) if b + 1 < items // ROWS else zeros
                before = pltpu.roll(read(b - 1), tracers, axis=0) if b else zeros
                return jnp.where(wide < tracers, turned, after) - jnp.where(
                    wide < tracers, before, turned
                )

            return tilt

        def own_row(n):
            return lambda b: own_lat[n, b * ROWS : (b + 1) * ROWS, :]

        def ghost_row(ref):
            return lambda b: ref[b * ROWS : (b + 1) * ROWS, :]

        for b in range(items // ROWS):
            at = slice(b * ROWS, (b + 1) * ROWS)
            past = slice(items + b * ROWS, items + (b + 1) * ROWS)
            level = (wide + b * ROWS) // tracers

            def mask(row):
                return jnp.where(level < jnp.broadcast_to(row, (ROWS, cols)), 1.0, 0.0)

            def coef(n):
                return spread_rows(own_lat_coef.at[n], 0, b)

            def ghost_mask(ref):
                row = ref[base + 3 * levels : base + 3 * levels + 1, :]
                return jnp.where(level.astype(F32) < jnp.broadcast_to(row, (ROWS, cols)), 1.0, 0.0)

            south_mask = jnp.where(lat > 0, ghost_mask(south), 0.0)

            def run(reads, j0, j3, open1, open2, d, v, s):
                tilts = [tilt_rows_of(r)(b) for r in reads]
                values = [r(b) for r in reads]
                lookup = dict(zip(map(id, values), tilts))
                return edge_faces(*values, j0, j3, open1, open2, *d, *v, *s,
                                  lambda x: lookup[id(x)])

            m0, m1 = mask(bottom[0:1, :]), mask(bottom[1:2, :])
            f0, f1 = run(
                (ghost_row(south), own_row(0), own_row(1)),
                jnp.where(lat > 0, south[past, :], 0.0), own_lat[2, at, :], south_mask * m0, m0 * m1,
                (spread_rows(south, base, b), coef(0), coef(1)),
                (spread_rows(south, base + levels, b), coef(4)),
                (spread_rows(south, base + 2 * levels, b), coef(7)),
            )
            fix_lat[0, at, :] = (f1 - f0) * m0
            fix_lat[1, at, :] = -f1 * m1
            m0 = mask(bottom[rows - 2 : rows - 1, :])
            m1 = mask(bottom[rows - 1 : rows, :])
            top_vel = coef(6)
            ghost_vel = spread_rows(north, base + levels, b)
            top_vel = jnp.where(top, 0.5 * (top_vel - ghost_vel), top_vel)
            f0, f1 = run(
                (own_row(3), own_row(4), ghost_row(north)),
                own_lat[5, at, :], sign * north[past, :], m0 * m1, m1 * ghost_mask(north),
                (coef(2), coef(3), spread_rows(north, base, b)),
                (coef(5), top_vel),
                (coef(8), coef(9)),
            )
            fix_lat[2, at, :] = f0 * m0
            fix_lat[3, at, :] = (f1 - f0) * m1

    edges()

    def one_block(step, side):
        at = rows_of(step)
        fetch(step).wait()

        def value_at(t, k, h):
            if not side:
                return explicit[t, k, at, h]
            n = k * tracers + t
            row0 = jnp.where(step == 0, 0, ROWS - 2)
            pick = jnp.where(step == 0, 0, 2)
            low = jnp.broadcast_to(fix_lat[pick, n : n + 1, h], (ROWS, LANES))
            high = jnp.broadcast_to(fix_lat[pick + 1, n : n + 1, h], (ROWS, LANES))
            return explicit[t, k, at, h] + jnp.where(
                sub == row0, low, jnp.where(sub == row0 + 1, high, 0.0)
            )

        depth = tuple(bottom[at, h] for h in halves)
        for i, h in enumerate(halves):
            ratio = above = None
            for k in range(levels):
                if k + 1 < levels:
                    below = jnp.where(depth[i] > k + 1, vertical[k, at, h], 0.0)
                if k == 0:
                    pivot = 1.0 + below
                elif k + 1 < levels:
                    pivot = (1.0 + above + below) + above * ratio
                else:
                    pivot = (1.0 + above) + above * ratio
                inverse = 1.0 / pivot
                pivots[0, k, :, h] = inverse
                if k:
                    pivots[1, k, :, h] = above
                if k + 1 < levels:
                    ratio = below * inverse
                    pivots[2, k, :, h] = ratio
                    above = below

        fixes = [fix_lon[i, at, :] for i in range(2)]
        for t in range(tracers):
            for i, h in enumerate(halves):
                begin = 0 if i == 0 else LANES - 2
                near = lane < 2 if i == 0 else lane >= LANES - 2
                values = []
                value = None
                for k in range(levels):
                    turn = (begin - 2 * (k * tracers + t)) % LANES
                    patch = pltpu.roll(fixes[i], turn, axis=1) if turn else fixes[i]
                    right = value_at(t, k, h) + jnp.where(near, patch, 0.0)
                    right = jnp.where(depth[i] > k, right, 0.0)
                    if k:
                        right = right + pivots[1, k, :, h] * value
                    value = right * pivots[0, k, :, h]
                    values.append(value)
                nxt = values[-1]
                field[t, levels - 1, at, h] = nxt
                for k in range(levels - 2, -1, -1):
                    nxt = values[k] + pivots[2, k, :, h] * nxt
                    field[t, k, at, h] = nxt
        store(step).start()

    @pl.loop(0, 2)
    def _(n):
        one_block(n * (blocks - 1), True)

    @pl.loop(1, blocks - 1)
    def _(step):
        one_block(step, False)

    for b in range(blocks):
        store(b).wait()


def solve(explicit, vertical, bottom, got, own):
    tracers, levels, rows, cols = explicit.shape
    items = levels * tracers
    lat_rows = got[0].shape[0]
    lat_count = lax.axis_size("lat")
    blocks = rows // ROWS

    def body(*refs):
        solve_kernel(levels, tracers, rows, cols, "lon", "lat", lat_count, *refs)

    hbm = pl.BlockSpec(memory_space=pltpu.HBM)
    vmem = pl.BlockSpec(memory_space=pltpu.VMEM)
    return pl.pallas_call(
        body,
        name="edges_and_solve",
        in_specs=[vmem, hbm] + [vmem] * 8,
        out_specs=hbm,
        out_shape=jax.ShapeDtypeStruct(explicit.shape, F32),
        scratch_shapes=[
            pltpu.VMEM(explicit.shape, F32),
            pltpu.VMEM(vertical.shape, F32),
            pltpu.VMEM((2, rows, LANES), F32),
            pltpu.VMEM((4, items, cols), F32),
            pltpu.VMEM((lat_rows, cols), F32),
            pltpu.VMEM((lat_rows, cols), F32),
            pltpu.VMEM((3, levels, ROWS, cols), F32),
            pltpu.SemaphoreType.DMA((blocks,)),
            pltpu.SemaphoreType.DMA((blocks,)),
        ],
        compiler_params=pltpu.CompilerParams(vmem_limit_bytes=SOLVE_LIMIT),
        cost_estimate=pl.CostEstimate(
            flops=20 * explicit.size, bytes_accessed=8 * 10**6, transcendentals=0
        ),
    )(explicit, vertical, bottom, *got, *own)


def local(
    tracer,
    east_velocity,
    north_velocity,
    diffusivity,
    east_slope,
    north_slope,
    vertical_diffusivity,
    sea_mask,
    bottom,
):
    lon, lat = lax.axis_size("lon"), lax.axis_size("lat")
    args = tuple(
        pltpu.with_memory_space_constraint(x, pltpu.HBM)
        for x in (
            tracer, east_velocity, north_velocity, diffusivity, east_slope, north_slope, bottom
        )
    )
    pay_a, pay_b, pay_c, pay_d, *kept = pack(*args)
    own, (held, held_vel, held_diff, held_slope, depth) = kept[:3], kept[3:8]
    north_vel, north_slope, open_at, *state = kept[8:]

    def swap(pairs):
        return [p for a, b in pairs for p in ((a, b), (b, a))]

    def at(i, j):
        return i * lat + j

    near_lat = swap([(j, j + 1) for j in range(0, lat, 2)])
    far_lat = swap([(at(i, j), at(i, j + 1)) for i in range(lon) for j in range(1, lat - 1, 2)])
    far_lat += [(at(i, lat - 1), at(lon - 1 - i, lat - 1)) for i in range(lon)]
    far_lat += swap([(at(i, 0), at(i + 1, 0)) for i in range(0, lon, 2)])
    near_lon = swap([(i, i + 1) for i in range(0, lon, 2)])
    far_lon = swap([(i, (i + 1) % lon) for i in range(1, lon, 2)])
    got_a = lax.ppermute(pay_a, "lat", near_lat)
    got_c = lax.ppermute(pay_c, "lon", near_lon)
    got_b = lax.ppermute(pay_b, ("lon", "lat"), far_lat)
    got_d = lax.ppermute(pay_d, "lon", far_lon)
    explicit = interior_rest(
        (held, held_vel, north_vel, held_diff, held_slope, north_slope, depth, open_at), state
    )
    return solve(
        explicit, vertical_diffusivity, depth, (got_a, got_b, got_c, got_d), tuple(own)
    )


def solution(mesh):
    field = P(None, "lat", "lon")
    placed = (
        P(None, None, "lat", "lon"),
        field,
        field,
        field,
        field,
        field,
        field,
        field,
        P("lat", "lon"),
    )
    return jax.shard_map(
        local, mesh=mesh, in_specs=placed, out_specs=P(None, None, "lat", "lon"), check_vma=False
    )
```
